32 devices in a mesh: seq: 8 (over z, y), fsdp: 4 (over x, core).
Axes of the slice: x: 2, y: 2, z: 4, core: 2. Of those that a mesh axis runs over, the one named last changes fastest.
Arguments:
- patches: bfloat16 [32, 1472, 1152], P('fsdp', 'seq'), may hold values from -6 to 6
- key_mask: int32 [32, 1472], P('fsdp'), may hold values from 0 to 1, as said below
- attn_norm_gain: bfloat16 [1152], P('fsdp'), may hold values from 0.5 to 1.5
- attn_norm_bias: bfloat16 [1152], P('fsdp'), may hold values from -3 to 3
- query_weight: bfloat16 [1152, 1152], P('fsdp'), may hold values from -0.1875 to 0.1875
- query_bias: bfloat16 [1152], P('fsdp'), may hold values from -3 to 3
- key_weight: bfloat16 [1152, 1152], P('fsdp'), may hold values from -0.1875 to 0.1875
- value_weight: bfloat16 [1152, 1152], P('fsdp'), may hold values from -0.1875 to 0.1875
- value_bias: bfloat16 [1152], P('fsdp'), may hold values from -3 to 3
- out_weight: bfloat16 [1152, 1152], P('fsdp'), may hold values from -1.5 to 1.5
- out_bias: bfloat16 [1152], P('fsdp'), may hold values from -3 to 3
- mlp_norm_gain: bfloat16 [1152], P('fsdp'), may hold values from 0.5 to 1.5
- mlp_norm_bias: bfloat16 [1152], P('fsdp'), may hold values from -3 to 3
- up_weight: bfloat16 [1152, 4304], P('fsdp'), may hold values from -0.1875 to 0.1875
- up_bias: bfloat16 [4304], P('fsdp'), may hold values from -3 to 3
- down_weight: bfloat16 [4304, 1152], P(None, 'fsdp'), may hold values from -0.09375 to 0.09375
- down_bias: bfloat16 [1152], P('fsdp'), may hold values from -3 to 3
- cotangent: bfloat16 [32, 1472, 1152], P('fsdp', 'seq'), may hold values from -6 to 6
Outputs:
- output: bfloat16 [32, 1472, 1152], P('fsdp', 'seq')
- input_grad: bfloat16 [32, 1472, 1152], P('fsdp', 'seq')
- attn_norm_gain_grad: float32 [1152], P('fsdp')
- attn_norm_bias_grad: float32 [1152], P('fsdp')
- query_weight_grad: float32 [1152, 1152], P('fsdp')
- query_bias_grad: float32 [1152], P('fsdp')
- key_weight_grad: float32 [1152, 1152], P('fsdp')
- value_weight_grad: float32 [1152, 1152], P('fsdp')
- value_bias_grad: float32 [1152], P('fsdp')
- out_weight_grad: float32 [1152, 1152], P('fsdp')
- out_bias_grad: float32 [1152], P('fsdp')
- mlp_norm_gain_grad: float32 [1152], P('fsdp')
- mlp_norm_bias_grad: float32 [1152], P('fsdp')
- up_weight_grad: float32 [1152, 4304], P('fsdp')
- up_bias_grad: float32 [4304], P('fsdp')
- down_weight_grad: float32 [4304, 1152], P(None, 'fsdp')
- down_bias_grad: float32 [1152], P('fsdp')
The draws below stay inside these ranges and needn't reach their ends.
Inputs may be any that keep to these rules, and one draw needn't show every extreme that they name: `key_mask`: in each image (each run of 736 positions of a row) exactly 729 positions hold 1 and the others 0.
All inputs are finite; a program needn't handle non-finite values.
Results may differ from the reference program's by a relative error of at most 0.019.
Values may be sent and summed in bfloat16 or wider, within the bound.
No kernel may reach another device: no remote copies, remote signals or barrier semaphores. Data moves between devices by JAX's collectives and lax.ppermute only.
A program may use at most 320 MiB of HBM per device.

```python
import math
import jax
import jax.numpy as jnp
from jax import lax

D = 1152
H = 16
HD = 72
FF = 4304
VALID = 729
SEQ = 736
PACK = 2
IMAGES = 64
ROWS = 32


def draw_key_mask(key, part):
    image_keys = jax.random.split(jax.random.fold_in(key, 7), IMAGES)

    def one_image(image_key):
        order = jax.random.permutation(image_key, SEQ)
        return jnp.where(order < SEQ - VALID, 0, 1).astype(jnp.int32)
    return jax.vmap(one_image)(image_keys).reshape(ROWS, PACK * SEQ)


def with_spikes(drawn, key, source, target, blocks, factor):
    owner, partner = [(jnp.arange(drawn.shape[axis_at]) // (drawn.shape[axis_at] // blocks)).reshape([-1 if axis == axis_at else 1 for axis in range(drawn.ndim)]) for axis_at in (source, target)]
    chosen = jax.random.permutation(key, blocks)[partner]
    strong = (owner == chosen) | (owner == (partner + blocks // 2) % blocks)
    return jnp.where(strong, factor * drawn, drawn)


def levels(stream_key, shape, pieces, low, top_value):
    loudness = 1.0
    for position, blocks in pieces:
        draws = jax.random.uniform(jax.random.fold_in(jax.random.fold_in(stream_key, 6), position), (blocks,), jnp.float32, low / len(pieces), top_value / len(pieces))
        loudness = loudness * jnp.repeat(jnp.exp(draws), shape[position] // blocks).reshape((-1,) + (1,) * (len(shape) - 1 - position))
    return loudness


def normal_values(stream_key, dims, scale, bound, cuts=(), held_as=jnp.bfloat16):
    array = jax.random.normal(stream_key, dims, jnp.float32) * scale
    if len(cuts) > 0:
        array = levels(stream_key, dims, cuts, -0.22, 0.18) * array
    return jnp.clip(array, min=-bound, max=bound).astype(held_as)


def noise_with(stream_key, shape, scale, limit, cuts, heavy, held_as=jnp.bfloat16):
    drawn = scale * jax.random.normal(stream_key, shape, jnp.float32)
    if cuts:
        drawn = drawn * levels(stream_key, shape, cuts, -0.22, 0.18)
    return jnp.clip(with_spikes(drawn, jax.random.fold_in(stream_key, 3), *heavy), -limit, limit).astype(held_as)


def setup_inputs(seed: int = 0) -> dict:
    key_list = jax.random.split(jax.random.key(seed), 19)
    patches = normal_values(key_list[0], (ROWS, PACK * SEQ, D), 1.0, 6.0, ((0, 4), (1, 8)))
    key_mask = draw_key_mask(jax.random.fold_in(key_list[18], 71), 0)
    attn_norm_gain = jnp.clip(1.0 + 0.1 * jax.random.normal(key_list[2], (D,), jnp.float32), 0.5, 1.5).astype(jnp.bfloat16)
    attn_norm_bias = normal_values(key_list[3], (D,), 0.5, 3.0, ((0, 4),))
    query_weight = normal_values(key_list[4], (D, D), D ** -0.5, 0.1875, ((0, 4),))
    query_bias = normal_values(key_list[5], (D,), 0.5, 3.0, ((0, 4),))
    key_weight = normal_values(key_list[6], (D, D), D ** -0.5, 0.1875, ((0, 4),))
    value_weight = normal_values(key_list[7], (D, D), D ** -0.5, 0.1875, ((0, 4),))
    value_bias = normal_values(key_list[8], (D,), 0.5, 3.0, ((0, 4),))
    out_weight = normal_values(key_list[9], (D, D), (max(D // 64, 1)) ** -0.5, 1.5, ((0, 4),))
    out_bias = normal_values(key_list[10], (D,), 0.5, 3.0, ((0, 4),))
    mlp_norm_gain = jnp.clip(1.0 + 0.1 * jax.random.normal(key_list[11], (D,), jnp.float32), 0.5, 1.5).astype(jnp.bfloat16)
    mlp_norm_bias = normal_values(key_list[12], (D,), 0.5, 3.0, ((0, 4),))
    up_weight = normal_values(key_list[13], (D, FF), D ** -0.5, 0.1875, ((0, 4),))
    up_bias = normal_values(key_list[14], (FF,), 0.5, 3.0, ((0, 4),))
    down_weight = normal_values(key_list[15], (FF, D), FF ** -0.5, 0.09375, ((1, 4),))
    down_bias = normal_values(key_list[16], (D,), 0.5, 3.0, ((0, 4),))
    cotangent = noise_with(key_list[17], (ROWS, PACK * SEQ, D), 1.0, 6.0, ((0, 4), (1, 8)), (0, 2, 4, 2.0))
    return dict(patches=patches, key_mask=key_mask, attn_norm_gain=attn_norm_gain, attn_norm_bias=attn_norm_bias, query_weight=query_weight, query_bias=query_bias, key_weight=key_weight, value_weight=value_weight, value_bias=value_bias, out_weight=out_weight, out_bias=out_bias, mlp_norm_gain=mlp_norm_gain, mlp_norm_bias=mlp_norm_bias, up_weight=up_weight, up_bias=up_bias, down_weight=down_weight, down_bias=down_bias, cotangent=cotangent)


epsilon = 1e-06
highest = lax.Precision.HIGHEST

@jax.custom_vjp
def low(v):
    return lax.optimization_barrier(v.astype(jnp.bfloat16)).astype(jnp.float32)

@jax.custom_vjp
def low_back(v):
    return v

def low_keep(v):
    return (low(v), None)

def low_pass(kept, grad):
    return (grad,)

def back_keep(v):
    return (v, None)

def back_low(kept, grad):
    return (low(grad),)
low.defvjp(low_keep, low_pass)
low_back.defvjp(back_keep, back_low)

def layer_norm(values, norm_gain, norm_shift):
    center = values - lax.optimization_barrier(jnp.mean(values, -1, keepdims=True))
    spread = lax.optimization_barrier(jnp.mean(center * center, -1, keepdims=True))
    return center * lax.rsqrt(spread + epsilon) * norm_gain + norm_shift

def project(left_side, right_side):
    return jnp.einsum('gsd,de->gse', left_side, right_side, precision=highest)

def layer_block(params, inputs, mask_group):
    first_gain, first_shift, query_full, query_shift, key_full, value_full, value_shift, out_full, out_shift, second_gain, second_shift, up_full, up_shift, down_full, down_shift = params
    groups = inputs.shape[0]
    length = inputs.shape[1]
    model_width = inputs.shape[2]
    normed = low(layer_norm(inputs, first_gain, first_shift))
    queries = low(low_back(project(normed, query_full) + query_shift)).reshape(groups, length, H, HD)
    key_rows = low(low_back(project(normed, key_full))).reshape(groups, length, H, HD)
    value_rows = low(low_back(project(normed, value_full) + value_shift)).reshape(groups, length, H, HD)
    raw_scores = jnp.einsum('gqhd,gkhd->ghqk', queries, key_rows, precision=highest)
    scores = low_back(raw_scores) * (1.0 / math.sqrt(HD))
    masked = jnp.where(mask_group[:, None, None, :] > 0, scores, -1e+30)
    attn_probs = jax.nn.softmax(masked, axis=-1)
    context = jnp.einsum('ghqk,gkhd->gqhd', low(attn_probs), value_rows, precision=highest)
    context = low(low_back(context.reshape(groups, length, model_width)))
    attended = low_back(project(context, out_full) + out_shift)
    hidden = inputs + attended
    normed_two = low(layer_norm(hidden, second_gain, second_shift))
    preact = low_back(project(normed_two, up_full) + up_shift)
    active = low(jax.nn.gelu(preact, approximate=True))
    branch = low_back(project(active, down_full) + down_shift)
    return hidden + branch

def reference(patches, key_mask, attn_norm_gain, attn_norm_bias, query_weight, query_bias, key_weight, value_weight, value_bias, out_weight, out_bias, mlp_norm_gain, mlp_norm_bias, up_weight, up_bias, down_weight, down_bias, cotangent):
    params = tuple((tensor.astype(jnp.float32) for tensor in (attn_norm_gain, attn_norm_bias, query_weight, query_bias, key_weight, value_weight, value_bias, out_weight, out_bias, mlp_norm_gain, mlp_norm_bias, up_weight, up_bias, down_weight, down_bias)))
    inputs = patches.astype(jnp.float32)
    image_mask = key_mask.reshape(IMAGES, SEQ)

    def forward(values, weights):
        grouped = values.reshape(IMAGES // 4, 4, SEQ, D)
        mask_groups = image_mask.reshape(IMAGES // 4, 4, SEQ)

        def one_group(bundle):
            return jax.checkpoint(layer_block)(weights, bundle[0], bundle[1])
        return lax.map(one_group, (grouped, mask_groups)).reshape(ROWS, PACK * SEQ, D)
    output, pullback = jax.vjp(forward, inputs, params)
    incoming = cotangent.astype(jnp.float32) * key_mask[:, :, None].astype(jnp.float32)
    input_grad, weight_grads = pullback(incoming)
    return (output.astype(jnp.bfloat16), input_grad.astype(jnp.bfloat16), weight_grads[0], weight_grads[1], weight_grads[2], weight_grads[3], weight_grads[4], weight_grads[5], weight_grads[6], weight_grads[7], weight_grads[8], weight_grads[9], weight_grads[10], weight_grads[11], weight_grads[12], weight_grads[13], weight_grads[14])
```

```python
import functools
import math

import jax
import jax.numpy as jnp
from jax import lax
from jax.experimental import pallas as pl
from jax.experimental.pallas import tpu as pltpu
from jax.sharding import PartitionSpec as P

HD = 72
SEQ = 736
EPS = 1e-06
SCALE = 1.0 / math.sqrt(HD)
SCALE_LOG2 = SCALE * math.log2(math.e)
QUERY_BLOCK = 736

f32 = jnp.float32
bf16 = jnp.bfloat16


def dot2(a, b, ca, cb):
    return lax.dot_general(a, b, (((ca,), (cb,)), ((), ())), preferred_element_type=f32)


def split3(v):
    high = v.astype(bf16).astype(f32)
    mid = (v - high).astype(bf16).astype(f32)
    return [high, mid, v - high - mid]


def rows8(rows, length):
    row = lax.broadcasted_iota(jnp.int32, (8, length), 0)
    out = jnp.zeros((8, length), f32)
    for j, value in enumerate(rows):
        out = jnp.where(row == j, value, out)
    return out


def query_blocks(length):
    return [(s, min(QUERY_BLOCK, length - s)) for s in range(0, length, QUERY_BLOCK)]


def attend_forward_kernel(q_ref, k_ref, v_ref, mask_ref, context_ref, lse_ref):
    length = q_ref.shape[-1]
    keys = k_ref[0].astype(f32)
    bias = jnp.where(mask_ref[0] > 0, 0.0, -1e30).astype(f32)
    one = jnp.ones((1, length), f32)
    zeros = jnp.zeros((8, length), f32)
    key_side = jnp.concatenate([keys, rows8([bias], length), keys, zeros], 0).T.astype(bf16)
    scaled = q_ref[0].astype(f32) * SCALE_LOG2
    high = scaled.astype(bf16).astype(f32)
    query_side = jnp.concatenate([high, rows8([one], length), scaled - high, zeros], 0).astype(bf16)
    value_side = jnp.concatenate([v_ref[0].astype(f32), jnp.ones((8, length), f32)], 0).astype(bf16)
    for s, n in query_blocks(length):
        scores = dot2(key_side, query_side[:, s : s + n], 1, 0)
        top = jnp.max(scores, 0, keepdims=True)
        probs = jnp.exp2(scores - top).astype(bf16)
        summed = dot2(value_side, probs, 1, 0)
        total = summed[HD : HD + 1]
        context_ref[0, :, s : s + n] = (summed[:HD] * (1.0 / total)).astype(bf16)
        lse_ref[0, 0, :, s : s + n] = top + jnp.log2(total)


def attend_forward(queries, keys, values, mask):
    images, width, length = queries.shape
    heads = width // HD
    block = pl.BlockSpec((1, HD, length), lambda i, h: (i, h, 0))
    return pl.pallas_call(
        attend_forward_kernel,
        grid=(images, heads),
        in_specs=[block, block, block, pl.BlockSpec((1, 1, length), lambda i, h: (i, 0, 0))],
        out_specs=[block, pl.BlockSpec((1, 1, 1, length), lambda i, h: (i, h, 0, 0))],
        out_shape=[
            jax.ShapeDtypeStruct((images, width, length), bf16),
            jax.ShapeDtypeStruct((images, heads, 1, length), f32),
        ],
        compiler_params=pltpu.CompilerParams(vmem_limit_bytes=50 << 20),
        cost_estimate=pl.CostEstimate(
            flops=images * heads * length * length * 1024,
            bytes_accessed=images * width * length * 8,
            transcendentals=images * heads * length * length,
        ),
        name="attend_forward",
    )(queries, keys, values, mask)


def attend_backward_kernel(
    q_ref, k_ref, v_ref, context_ref, grad_ref, lse_ref, mask_ref, dq_ref, dk_ref, dv_ref
):
    length = q_ref.shape[-1]
    key_low = k_ref[0]
    keys = key_low.astype(f32)
    bias = jnp.where(mask_ref[0] > 0, 0.0, -1e30).astype(f32)
    one = jnp.ones((1, length), f32)
    zeros = jnp.zeros((8, length), f32)
    key_side = jnp.concatenate(
        [keys, rows8([bias, one, one, one], length), keys, zeros], 0
    ).T.astype(bf16)
    queries = q_ref[0].astype(f32)
    scaled = queries * SCALE_LOG2
    high = scaled.astype(bf16).astype(f32)
    query_side = jnp.concatenate(
        [high, rows8([one] + split3(-lse_ref[0, 0]), length), scaled - high, zeros], 0
    ).astype(bf16)
    grads = grad_ref[0].astype(f32)
    row_dot = jnp.sum(grads * context_ref[0].astype(f32), 0, keepdims=True)
    grad_side = jnp.concatenate([grads, rows8(split3(-row_dot), length)], 0).astype(bf16)
    value_side = jnp.concatenate(
        [v_ref[0].astype(f32), rows8([one, one, one], length)], 0
    ).T.astype(bf16)
    query_rows = queries.T.astype(bf16)
    grad_rows = grads.T.astype(bf16)
    dk = jnp.zeros((length, HD), f32)
    dv = jnp.zeros((length, HD), f32)
    for s, n in query_blocks(length):
        probs = jnp.exp2(dot2(key_side, query_side[:, s : s + n], 1, 0))
        prob_grads = dot2(value_side, grad_side[:, s : s + n], 1, 0)
        score_grads = (probs * prob_grads).astype(bf16)
        dv += dot2(probs.astype(bf16), grad_rows[s : s + n], 1, 0)
        dk += dot2(score_grads, query_rows[s : s + n], 1, 0)
        dq_ref[0, :, s : s + n] = (dot2(key_low, score_grads, 1, 0) * SCALE).astype(bf16)
    dk_ref[0] = (dk * SCALE).T.astype(bf16)
    dv_ref[0] = dv.T.astype(bf16)


def attend_backward(queries, keys, values, context, grads, lse, mask):
    images, width, length = queries.shape
    heads = width // HD
    block = pl.BlockSpec((1, HD, length), lambda i, h: (i, h, 0))
    out = jax.ShapeDtypeStruct((images, width, length), bf16)
    return pl.pallas_call(
        attend_backward_kernel,
        grid=(images, heads),
        in_specs=[block] * 5
        + [
            pl.BlockSpec((1, 1, 1, length), lambda i, h: (i, h, 0, 0)),
            pl.BlockSpec((1, 1, length), lambda i, h: (i, 0, 0)),
        ],
        out_specs=[block] * 3,
        out_shape=[out, out, out],
        compiler_params=pltpu.CompilerParams(vmem_limit_bytes=50 << 20),
        cost_estimate=pl.CostEstimate(
            flops=images * heads * length * length * 2560,
            bytes_accessed=images * width * length * 16,
            transcendentals=images * heads * length * length,
        ),
        name="attend_backward",
    )(queries, keys, values, context, grads, lse, mask)


def swap(values, axis, bits):
    return lax.ppermute(values, axis, [(i, i ^ bits) for i in range(lax.axis_size(axis))])


def take_block(values, index, size):
    return lax.dynamic_slice_in_dim(values, index * size, size, 0)


def tokens_to_images(tokens, member, group):
    share = tokens.shape[0] // group
    blocks = [take_block(tokens, member ^ j, share) for j in range(group)]
    return jnp.concatenate(
        [blocks[0]] + [swap(blocks[j], "seq", j) for j in range(1, group)], axis=1
    )


def images_to_tokens(images, member, group):
    share, length, width = images.shape
    local = length // group
    out = jnp.zeros((share * group, local, width), images.dtype)
    for j in range(group):
        block = images[:, j * local : (j + 1) * local]
        if j:
            block = swap(block, "seq", j)
        out = lax.dynamic_update_slice_in_dim(out, block, (member ^ j) * share, 0)
    return out


def gather_small(local):
    me = lax.axis_index("fsdp")
    count = lax.axis_size("fsdp")
    held = local[None]
    bit = 1
    while bit < count:
        held = jnp.concatenate([held, swap(held, "fsdp", bit)], 0)
        bit *= 2
    return jnp.concatenate([take_block(held, me ^ j, 1) for j in range(count)], 0)


def sum_everywhere(values):
    for axis in ("fsdp", "seq"):
        bit = 1
        while bit < lax.axis_size(axis):
            values = values + swap(values, axis, bit)
            bit *= 2
    return values


def merge(mine, other, bit):
    return jnp.where(
        bit == 0, jnp.concatenate([mine, other], 0), jnp.concatenate([other, mine], 0)
    )


def sum_seq(values, order):
    me = lax.axis_index("seq")
    halved = []
    for step in order:
        rows = values.shape[0]
        bit = (me // step) % 2
        if rows % 16 == 0 and step != order[-1]:
            half = rows // 2
            sent = take_block(values, 1 - bit, half)
            kept = take_block(values, bit, half)
            halved.append((step, bit))
        else:
            sent = kept = values
        values = (kept.astype(f32) + swap(sent, "seq", step).astype(f32)).astype(bf16)
    for step, bit in reversed(halved):
        values = merge(values, swap(values, "seq", step), bit)
    return values


def seq_bits():
    bits, bit = [], 1
    while bit < lax.axis_size("seq"):
        bits.append(bit)
        bit *= 2
    return bits


def own_grad(full, order):
    mine = lax.psum_scatter(full.astype(bf16), "fsdp", scatter_dimension=0, tiled=True)
    return sum_seq(mine, order).astype(f32)


def norm_parts(values):
    center = values - jnp.mean(values, -1, keepdims=True)
    spread = jnp.mean(center * center, -1, keepdims=True)
    scale = lax.rsqrt(spread + EPS)
    return center * scale, scale


def norm_grad(grad, hat, scale, gain):
    e = grad * gain
    return scale * (
        e - jnp.mean(e, -1, keepdims=True) - hat * jnp.mean(e * hat, -1, keepdims=True)
    )


def ein(spec, a, b):
    return jnp.einsum(spec, a, b, preferred_element_type=f32)


def token_sum(values):
    return jnp.sum(values.astype(f32), (0, 1))


def body(
    patches,
    key_mask,
    attn_norm_gain,
    attn_norm_bias,
    query_weight,
    query_bias,
    key_weight,
    value_weight,
    value_bias,
    out_weight,
    out_bias,
    mlp_norm_gain,
    mlp_norm_bias,
    up_weight,
    up_bias,
    down_weight,
    down_bias,
    cotangent,
):
    rows, local, width = patches.shape
    group = SEQ // local
    share = rows // group
    shard = lax.axis_index("fsdp")
    seq = lax.axis_index("seq")
    member = seq % group
    bits = seq_bits()
    order_a = bits
    order_b = [bits[1], bits[0]] + bits[2:] if len(bits) > 1 else bits

    inputs_low = tokens_to_images(patches, member, group)

    small = [
        attn_norm_gain,
        attn_norm_bias,
        query_bias,
        value_bias,
        out_bias,
        mlp_norm_gain,
        mlp_norm_bias,
        down_bias,
        up_bias,
    ]
    gathered = gather_small(jnp.concatenate(small)).astype(f32)
    starts = [0]
    for v in small:
        starts.append(starts[-1] + v.shape[0])
    (
        first_gain,
        first_shift,
        query_shift,
        value_shift,
        out_shift,
        second_gain,
        second_shift,
        down_shift,
        up_shift,
    ) = (gathered[:, a:b].reshape(-1) for a, b in zip(starts[:-1], starts[1:]))

    def whole(weight):
        return lax.all_gather(weight, "fsdp", axis=0, tiled=True)

    query_full = whole(query_weight)
    key_full = whole(key_weight)
    value_full = whole(value_weight)
    out_full = whole(out_weight)
    up_full = whole(up_weight)
    down_full = whole(down_weight.T)

    cotangent_low = tokens_to_images(cotangent, member, group)
    image_mask = lax.dynamic_slice(
        key_mask, (member * share, (seq // group) * SEQ), (share, SEQ)
    )
    image_mask = jnp.concatenate(
        [
            lax.dynamic_slice_in_dim(image_mask, (member ^ j) * local, local, 1)
            for j in range(group)
        ],
        axis=1,
    )
    key_keep = image_mask[:, None, :]

    inputs = inputs_low.astype(f32)
    hat_one, _ = norm_parts(inputs)
    normed_one = (hat_one * first_gain + first_shift).astype(bf16)
    queries = (ein("itd,dn->int", normed_one, query_full) + query_shift[:, None]).astype(bf16)
    keys = ein("itd,dn->int", normed_one, key_full).astype(bf16)
    values = (ein("itd,dn->int", normed_one, value_full) + value_shift[:, None]).astype(bf16)
    context, lse = attend_forward(queries, keys, values, key_keep)
    hidden = inputs + ein("int,nd->itd", context, out_full) + out_shift
    hat_two, scale_two = norm_parts(hidden)
    normed_two = (hat_two * second_gain + second_shift).astype(bf16)
    pre = ein("itd,df->itf", normed_two, up_full) + up_shift
    tanh = jnp.tanh(math.sqrt(2 / math.pi) * (pre + 0.044715 * pre * pre * pre))
    active = (0.5 * pre * (1.0 + tanh)).astype(bf16)
    slope = (
        0.5 * (1.0 + tanh)
        + 0.5
        * pre
        * (1.0 - tanh * tanh)
        * (math.sqrt(2 / math.pi) * (1.0 + 3 * 0.044715 * pre * pre))
    ).astype(bf16)
    output = (hidden + ein("itf,df->itd", active, down_full) + down_shift).astype(bf16)
    output = images_to_tokens(output, member, group)

    out_grad_low = jnp.where(image_mask[:, :, None] > 0, cotangent_low, 0).astype(bf16)
    down_grad = ein("itd,itf->df", out_grad_low, active)
    down_bias_grad = token_sum(out_grad_low)
    down_owned = own_grad(down_grad, order_a).T
    pre_grad = (ein("itd,df->itf", out_grad_low, down_full) * slope.astype(f32)).astype(bf16)
    up_grad = ein("itd,itf->df", normed_two, pre_grad)
    up_bias_grad = token_sum(pre_grad)
    up_owned = own_grad(up_grad, order_b)
    normed_two_grad = ein("itf,df->itd", pre_grad, up_full)
    hidden_grad = out_grad_low.astype(f32) + norm_grad(
        normed_two_grad, hat_two, scale_two, second_gain
    )
    second_gain_grad = jnp.sum(normed_two_grad * hat_two, (0, 1))
    second_shift_grad = jnp.sum(normed_two_grad, (0, 1))

    attn_grad_low = hidden_grad.astype(bf16)
    context_grad = ein("itd,nd->int", attn_grad_low, out_full).astype(bf16)
    out_grad = ein("int,itd->nd", context, attn_grad_low)
    out_bias_grad = token_sum(attn_grad_low)
    out_owned = own_grad(out_grad, order_a)
    dq, dk, dv = attend_backward(queries, keys, values, context, context_grad, lse, key_keep)
    query_owned = own_grad(ein("itd,int->dn", normed_one, dq), order_b)
    key_owned = own_grad(ein("itd,int->dn", normed_one, dk), order_a)
    value_owned = own_grad(ein("itd,int->dn", normed_one, dv), order_b)
    query_bias_grad = jnp.sum(dq.astype(f32), (0, 2))
    value_bias_grad = jnp.sum(dv.astype(f32), (0, 2))
    normed_one_grad = (
        ein("int,dn->itd", dq, query_full)
        + ein("int,dn->itd", dk, key_full)
        + ein("int,dn->itd", dv, value_full)
    )
    hat_one, scale_one = norm_parts(inputs_low.astype(f32))
    first_gain_grad = jnp.sum(normed_one_grad * hat_one, (0, 1))
    first_shift_grad = jnp.sum(normed_one_grad, (0, 1))
    input_grad = (
        hidden_grad + norm_grad(normed_one_grad, hat_one, scale_one, first_gain)
    ).astype(bf16)
    input_grad = images_to_tokens(input_grad, member, group)

    small_grads = [
        first_gain_grad,
        first_shift_grad,
        query_bias_grad,
        value_bias_grad,
        out_bias_grad,
        second_gain_grad,
        second_shift_grad,
        down_bias_grad,
        up_bias_grad,
    ]
    count = lax.axis_size("fsdp")
    packed = jnp.concatenate([v.reshape(count, -1) for v in small_grads], 1)
    packed = take_block(sum_everywhere(packed), shard, 1)[0]
    (
        first_gain_owned,
        first_shift_owned,
        query_bias_owned,
        value_bias_owned,
        out_bias_owned,
        second_gain_owned,
        second_shift_owned,
        down_bias_owned,
        up_bias_owned,
    ) = (packed[a:b] for a, b in zip(starts[:-1], starts[1:]))
    return (
        output,
        input_grad,
        first_gain_owned,
        first_shift_owned,
        query_owned,
        query_bias_owned,
        key_owned,
        value_owned,
        value_bias_owned,
        out_owned,
        out_bias_owned,
        second_gain_owned,
        second_shift_owned,
        up_owned,
        up_bias_owned,
        down_owned,
        down_bias_owned,
    )


def solution(mesh):
    tokens, vector, matrix = P("fsdp", "seq", None), P("fsdp"), P("fsdp", None)
    in_specs = (
        tokens,
        matrix,
        vector,
        vector,
        matrix,
        vector,
        matrix,
        matrix,
        vector,
        matrix,
        vector,
        vector,
        vector,
        matrix,
        vector,
        P(None, "fsdp"),
        vector,
        tokens,
    )
    out_specs = (
        tokens,
        tokens,
        vector,
        vector,
        matrix,
        vector,
        matrix,
        matrix,
        vector,
        matrix,
        vector,
        vector,
        vector,
        matrix,
        vector,
        P(None, "fsdp"),
        vector,
    )
    return jax.shard_map(body, mesh=mesh, in_specs=in_specs, out_specs=out_specs, check_vma=False)
```

```python
import math

import jax
import jax.numpy as jnp
from jax import lax
from jax.experimental import pallas as pl
from jax.experimental.layout import Layout, with_layout_constraint
from jax.experimental.pallas import tpu as pltpu
from jax.sharding import PartitionSpec as P

HD = 72
SEQ = 736
EPS = 1e-06
SCALE = 1.0 / math.sqrt(HD)
SCALE_LOG2 = SCALE * math.log2(math.e)
QUERY_BLOCK = 736
HEAD_GROUPS = ((0, 8), (8, 8))

GELU_A = math.sqrt(2 / math.pi)
GELU_B = 0.044715 * GELU_A

f32 = jnp.float32
bf16 = jnp.bfloat16


def dot2(a, b, ca, cb):
    return lax.dot_general(a, b, (((ca,), (cb,)), ((), ())), preferred_element_type=f32)


def split3(v):
    high = v.astype(bf16).astype(f32)
    mid = (v - high).astype(bf16).astype(f32)
    return [high, mid, v - high - mid]


def rows8(rows, length):
    row = lax.broadcasted_iota(jnp.int32, (8, length), 0)
    out = jnp.zeros((8, length), f32)
    for j, value in enumerate(rows):
        out = jnp.where(row == j, value, out)
    return out


def query_blocks(length):
    return [(s, min(QUERY_BLOCK, length - s)) for s in range(0, length, QUERY_BLOCK)]


def attend_forward_kernel(q_ref, k_ref, v_ref, mask_ref, context_ref, lse_ref):
    length = q_ref.shape[-1]
    keys = k_ref[0].astype(f32)
    bias = jnp.where(mask_ref[0] > 0, 0.0, -1e30).astype(f32)
    one = jnp.ones((1, length), f32)
    zeros = jnp.zeros((8, length), f32)
    key_side = jnp.concatenate([keys, rows8([bias], length), keys, zeros], 0).T.astype(bf16)
    scaled = q_ref[0].astype(f32) * SCALE_LOG2
    high = scaled.astype(bf16).astype(f32)
    query_side = jnp.concatenate([high, rows8([one], length), scaled - high, zeros], 0).astype(bf16)
    value_side = jnp.concatenate([v_ref[0].astype(f32), jnp.ones((8, length), f32)], 0).astype(bf16)
    for s, n in query_blocks(length):
        scores = dot2(key_side, query_side[:, s : s + n], 1, 0)
        top = jnp.max(scores, 0, keepdims=True)
        probs = jnp.exp2(scores - top).astype(bf16)
        summed = dot2(value_side, probs, 1, 0)
        total = summed[HD : HD + 1]
        context_ref[0, :, s : s + n] = (summed[:HD] * (1.0 / total)).astype(bf16)
        lse_ref[0, 0, :, s : s + n] = top + jnp.log2(total)


def attend_forward(projected, mask):
    images, features, length = projected.shape
    width = features // 3
    heads = width // HD
    block = pl.BlockSpec((1, HD, length), lambda i, h: (i, h, 0))
    sources = [
        pl.BlockSpec((1, HD, length), lambda i, h, which=which: (i, which * heads + h, 0))
        for which in range(3)
    ]
    return pl.pallas_call(
        attend_forward_kernel,
        grid=(images, heads),
        in_specs=sources + [pl.BlockSpec((1, 1, length), lambda i, h: (i, 0, 0))],
        out_specs=[block, pl.BlockSpec((1, 1, 1, length), lambda i, h: (i, h, 0, 0))],
        out_shape=[
            jax.ShapeDtypeStruct((images, width, length), bf16),
            jax.ShapeDtypeStruct((images, heads, 1, length), f32),
        ],
        compiler_params=pltpu.CompilerParams(vmem_limit_bytes=50 << 20),
        cost_estimate=pl.CostEstimate(
            flops=images * heads * length * length * 1024,
            bytes_accessed=images * width * length * 8,
            transcendentals=images * heads * length * length,
        ),
        name="attend_forward",
    )(projected, projected, projected, mask)


def attend_backward_kernel(
    q_ref,
    k_ref,
    v_ref,
    context_ref,
    grad_ref,
    lse_ref,
    mask_ref,
    *rest,
):
    all_ref, out_ref = rest[-2:]
    length = q_ref.shape[-1]
    key_low = k_ref[0]
    keys = key_low.astype(f32)
    bias = jnp.where(mask_ref[0] > 0, 0.0, -1e30).astype(f32)
    one = jnp.ones((1, length), f32)
    zeros = jnp.zeros((8, length), f32)
    key_side = jnp.concatenate(
        [keys, rows8([bias, one, one, one], length), keys, zeros], 0
    ).T.astype(bf16)
    queries = q_ref[0].astype(f32)
    scaled = queries * SCALE_LOG2
    high = scaled.astype(bf16).astype(f32)
    query_side = jnp.concatenate(
        [high, rows8([one] + split3(-lse_ref[0, 0]), length), scaled - high, zeros], 0
    ).astype(bf16)
    grads = grad_ref[0].astype(f32)
    row_dot = jnp.sum(grads * context_ref[0].astype(f32), 0, keepdims=True)
    grad_side = jnp.concatenate([grads, rows8(split3(-row_dot), length)], 0).astype(bf16)
    value_side = jnp.concatenate(
        [v_ref[0].astype(f32), rows8([one, one, one], length)], 0
    ).T.astype(bf16)
    query_rows = queries.T.astype(bf16)
    grad_rows = grads.T.astype(bf16)
    dk = jnp.zeros((length, HD), f32)
    dv = jnp.zeros((length, HD), f32)
    for s, n in query_blocks(length):
        probs = jnp.exp2(dot2(key_side, query_side[:, s : s + n], 1, 0))
        prob_grads = dot2(value_side, grad_side[:, s : s + n], 1, 0)
        score_grads = (probs * prob_grads).astype(bf16)
        dv += dot2(probs.astype(bf16), grad_rows[s : s + n], 1, 0)
        dk += dot2(score_grads, query_rows[s : s + n], 1, 0)
        dq = (dot2(key_low, score_grads, 1, 0) * SCALE).astype(bf16)
        out_ref[0, 0, :, s : s + n] = dq
        all_ref[0, 0, :, s : s + n] = dq
    for which, value in ((1, (dk * SCALE).T.astype(bf16)), (2, dv.T.astype(bf16))):
        out_ref[0, which] = value
        all_ref[0, which] = value


def attend_backward(projected, context, grads, lse, mask, first, count, held=None):
    images, features, length = projected.shape
    heads = features // (3 * HD)
    block = pl.BlockSpec((1, HD, length), lambda i, h: (i, first + h, 0))
    sources = [
        pl.BlockSpec((1, HD, length), lambda i, h, which=which: (i, which * heads + first + h, 0))
        for which in range(3)
    ]
    earlier = [] if held is None else [held]
    whole, part = pl.pallas_call(
        attend_backward_kernel,
        grid=(images, count),
        in_specs=sources
        + [
            block,
            block,
            pl.BlockSpec((1, 1, 1, length), lambda i, h: (i, first + h, 0, 0)),
            pl.BlockSpec((1, 1, length), lambda i, h: (i, 0, 0)),
        ]
        + [pl.BlockSpec(memory_space=pl.ANY)] * len(earlier),
        out_specs=[
            pl.BlockSpec((1, 3, HD, length), lambda i, h: (i, 0, first + h, 0)),
            pl.BlockSpec((1, 3, HD, length), lambda i, h: (i, 0, h, 0)),
        ],
        out_shape=[
            jax.ShapeDtypeStruct((images, 3, heads * HD, length), bf16),
            jax.ShapeDtypeStruct((images, 3, count * HD, length), bf16),
        ],
        input_output_aliases={7: 0} if earlier else {},
        compiler_params=pltpu.CompilerParams(vmem_limit_bytes=50 << 20),
        cost_estimate=pl.CostEstimate(
            flops=images * count * length * length * 2560,
            bytes_accessed=images * count * HD * length * 16,
            transcendentals=images * count * length * length,
        ),
        name="attend_backward",
    )(projected, projected, projected, context, grads, lse, mask, *earlier)
    return whole, part.reshape(images, 3 * count * HD, length)


def swap(values, axis, bits):
    return lax.ppermute(values, axis, [(i, i ^ bits) for i in range(lax.axis_size(axis))])


def take_block(values, index, size):
    return lax.dynamic_slice_in_dim(values, index * size, size, 0)


def tokens_to_images(tokens, member, group):
    share = tokens.shape[0] // group
    blocks = [take_block(tokens, member ^ j, share) for j in range(group)]
    return jnp.concatenate(
        [blocks[0]] + [swap(blocks[j], "seq", j) for j in range(1, group)], axis=1
    )


def images_to_tokens(images, member, group):
    share, length, width = images.shape
    local = length // group
    out = jnp.zeros((share * group, local, width), images.dtype)
    for j in range(group):
        block = images[:, j * local : (j + 1) * local]
        if j:
            block = swap(block, "seq", j)
        out = lax.dynamic_update_slice_in_dim(out, block, (member ^ j) * share, 0)
    return out


def gather_small(local):
    me = lax.axis_index("fsdp")
    count = lax.axis_size("fsdp")
    held = local[None]
    bit = 1
    while bit < count:
        held = jnp.concatenate([held, swap(held, "fsdp", bit)], 0)
        bit *= 2
    return jnp.concatenate([take_block(held, me ^ j, 1) for j in range(count)], 0)


def sum_chain(values):
    for axis in ("fsdp", "seq"):
        bit = 1
        while bit < lax.axis_size(axis):
            values, came = yield (values, swap(values, axis, bit))
            values = values + came
            bit *= 2
    return values


def merge(mine, other, bit):
    return jnp.where(
        bit == 0, jnp.concatenate([mine, other], 0), jnp.concatenate([other, mine], 0)
    )


def rows_first(values):
    return with_layout_constraint(values, Layout((0, 1)))


def reduce_chain(full, *orders):
    (values,) = yield (lax.psum_scatter(full, "fsdp", scatter_dimension=0, tiled=True),)
    me = lax.axis_index("seq")
    rows, width = values.shape
    cut = -(-width // (128 * len(orders))) * 128
    parts = [values[:, p * cut : min((p + 1) * cut, width)] for p in range(len(orders))]
    steps = len(orders[0])
    halved = []
    for k in range(steps):
        halve = rows % 16 == 0 and k < steps - 1
        flight = []
        for part, order in zip(parts, orders):
            sent = kept = part
            if halve:
                bit = (me // order[k]) % 2
                sent, kept = (take_block(part, b, rows // 2) for b in (1 - bit, bit))
            flight.append((kept, swap(sent, "seq", order[k])))
        flight = yield flight
        parts = [(kept.astype(f32) + came.astype(f32)).astype(bf16) for kept, came in flight]
        if halve:
            rows //= 2
            halved.append(k)
    for k in reversed(halved):
        flight = yield [
            (part, swap(part, "seq", order[k])) for part, order in zip(parts, orders)
        ]
        parts = [
            merge(part, came, (me // order[k]) % 2) for (part, came), order in zip(flight, orders)
        ]
    return jnp.concatenate(parts, 1)


class Flow:
    def __init__(self):
        self.chains, self.pending, self.results = {}, {}, {}

    def start(self, name, chain):
        self.chains[name], self.pending[name] = chain, next(chain)

    def point(self, main, *names):
        names = [name for name in names if name in self.pending]
        main, ended = lax.optimization_barrier((main, [self.pending[n] for n in names]))
        for name, values in zip(names, ended):
            self.advance(name, values)
        return main

    def advance(self, name, values):
        try:
            self.pending[name] = self.chains[name].send(values)
        except StopIteration as end:
            self.results[name] = end.value
            del self.pending[name]

    def finish(self):
        while self.pending:
            self.point((), *self.pending)


def seq_bits():
    bits, bit = [], 1
    while bit < lax.axis_size("seq"):
        bits.append(bit)
        bit *= 2
    return bits


def ungroup(parts, which):
    return jnp.concatenate(
        [
            part[..., which * heads * HD : (which + 1) * heads * HD]
            for part, (_, heads) in zip(parts, HEAD_GROUPS)
        ],
        -1,
    )


def norm_parts(values):
    center = values - jnp.mean(values, -1, keepdims=True)
    spread = jnp.mean(center * center, -1, keepdims=True)
    scale = lax.rsqrt(spread + EPS)
    return center * scale, scale


def norm_grad(grad, hat, scale, gain):
    e = grad * gain
    return scale * (
        e - jnp.mean(e, -1, keepdims=True) - hat * jnp.mean(e * hat, -1, keepdims=True)
    )


def ein(spec, a, b):
    return jnp.einsum(spec, a, b, preferred_element_type=f32)


def token_sum(values):
    return jnp.sum(values.astype(f32), (0, 1))


def body(
    patches,
    key_mask,
    attn_norm_gain,
    attn_norm_bias,
    query_weight,
    query_bias,
    key_weight,
    value_weight,
    value_bias,
    out_weight,
    out_bias,
    mlp_norm_gain,
    mlp_norm_bias,
    up_weight,
    up_bias,
    down_weight,
    down_bias,
    cotangent,
):
    rows, local, width = patches.shape
    group = SEQ // local
    share = rows // group
    shard = lax.axis_index("fsdp")
    seq = lax.axis_index("seq")
    member = seq % group
    bits = seq_bits()
    order_a = bits
    order_b = [bits[1], bits[0]] + bits[2:] if len(bits) > 1 else bits

    inputs_low = tokens_to_images(patches, member, group)

    small = [
        attn_norm_gain,
        attn_norm_bias,
        query_bias,
        value_bias,
        out_bias,
        mlp_norm_gain,
        mlp_norm_bias,
        down_bias,
        up_bias,
    ]
    gathered = gather_small(jnp.concatenate(small)).astype(f32)
    starts = [0]
    for v in small:
        starts.append(starts[-1] + v.shape[0])
    (
        first_gain,
        first_shift,
        query_shift,
        value_shift,
        out_shift,
        second_gain,
        second_shift,
        down_shift,
        up_shift,
    ) = (gathered[:, a:b].reshape(-1) for a, b in zip(starts[:-1], starts[1:]))

    def whole(weight):
        return lax.all_gather(weight, "fsdp", axis=0, tiled=True)

    project_full = whole(jnp.concatenate([query_weight, key_weight, value_weight], 1))
    project_shift = jnp.concatenate([query_shift, jnp.zeros_like(query_shift), value_shift])
    out_full = whole(out_weight)
    up_full = whole(up_weight)
    down_full = whole(down_weight.T)

    image_mask = lax.dynamic_slice(
        key_mask, (member * share, (seq // group) * SEQ), (share, SEQ)
    )
    image_mask = jnp.concatenate(
        [
            lax.dynamic_slice_in_dim(image_mask, (member ^ j) * local, local, 1)
            for j in range(group)
        ],
        axis=1,
    )
    key_keep = image_mask[:, None, :]

    inputs = inputs_low.astype(f32)
    hat_one, _ = norm_parts(inputs)
    normed_one = (hat_one * first_gain + first_shift).astype(bf16)
    projected = (ein("itd,dm->imt", normed_one, project_full) + project_shift[:, None]).astype(
        bf16
    )
    projected, cotangent = lax.optimization_barrier((projected, cotangent))
    cotangent_low = tokens_to_images(cotangent, member, group)
    context, lse = attend_forward(projected, key_keep)
    hidden = inputs + ein("int,nd->itd", context, out_full) + out_shift
    hat_two, scale_two = norm_parts(hidden)
    normed_two = (hat_two * second_gain + second_shift).astype(bf16)
    pre = ein("itd,df->itf", normed_two, up_full) + up_shift
    square = pre * pre
    tanh = jnp.tanh(pre * (GELU_A + GELU_B * square))
    half_pre = 0.5 * pre
    active, slope = lax.optimization_barrier(
        (
            (half_pre + half_pre * tanh).astype(bf16),
            (
                0.5 + 0.5 * tanh + half_pre * (1.0 - tanh * tanh) * (GELU_A + 3 * GELU_B * square)
            ).astype(bf16),
        )
    )
    flow = Flow()

    out_grad_low = jnp.where(image_mask[:, :, None] > 0, cotangent_low, 0).astype(bf16)
    down_grad = rows_first(ein("itd,itf->df", out_grad_low, active).astype(bf16))
    down_bias_grad = token_sum(out_grad_low)
    active, slope, out_grad_low, down_grad = flow.point((active, slope, out_grad_low, down_grad))
    flow.start("down", reduce_chain(down_grad, order_a, order_b))
    output = (hidden + ein("itf,df->itd", active, down_full) + down_shift).astype(bf16)
    output, slope = flow.point((output, slope))
    output = images_to_tokens(output, member, group)
    pre_grad = (ein("itd,df->itf", out_grad_low, down_full) * slope.astype(f32)).astype(bf16)
    up_bias_grad = token_sum(pre_grad)
    up_grad = rows_first(ein("itd,itf->df", normed_two, pre_grad).astype(bf16))
    pre_grad, up_grad = flow.point((pre_grad, up_grad))
    flow.start("up", reduce_chain(up_grad, order_a, order_b))
    normed_two_grad = ein("itf,df->itd", pre_grad, up_full)
    hidden_grad = out_grad_low.astype(f32) + norm_grad(
        normed_two_grad, hat_two, scale_two, second_gain
    )
    second_gain_grad = jnp.sum(normed_two_grad * hat_two, (0, 1))
    second_shift_grad = jnp.sum(normed_two_grad, (0, 1))
    hidden_grad, output = flow.point((hidden_grad, output), "down")

    attn_grad_low = hidden_grad.astype(bf16)
    context_grad = ein("itd,nd->int", attn_grad_low, out_full).astype(bf16)
    out_grad = rows_first(ein("int,itd->nd", context, attn_grad_low).astype(bf16))
    out_bias_grad = token_sum(attn_grad_low)
    context_grad, out_grad = flow.point((context_grad, out_grad))
    flow.start("out", reduce_chain(out_grad, order_a))
    grads, part_a = attend_backward(
        projected, context, context_grad, lse, key_keep, *HEAD_GROUPS[0]
    )
    grads, part_a, context_grad = flow.point((grads, part_a, context_grad), "down", "up")
    weight_grad = rows_first(ein("itd,imt->dm", normed_one, part_a).astype(bf16))
    weight_grad, grads, context_grad = flow.point(
        (weight_grad, grads, context_grad), "down", "up"
    )
    flow.start("a", reduce_chain(weight_grad, order_a, order_b))
    grads, part_b = attend_backward(
        projected, context, context_grad, lse, key_keep, *HEAD_GROUPS[1], grads
    )
    grads, part_b = flow.point((grads, part_b), "down", "up", "out")
    weight_grad = rows_first(ein("itd,imt->dm", normed_one, part_b).astype(bf16))
    grads, weight_grad = flow.point((grads, weight_grad), "down", "up", "out", "a")
    flow.start("b", reduce_chain(weight_grad, order_a, order_b))
    bias_grads = [jnp.sum(part.astype(f32), (0, 2)) for part in (part_a, part_b)]
    normed_one_grad = ein("imt,dm->itd", grads.reshape(projected.shape), project_full)
    query_bias_grad, value_bias_grad = ungroup(bias_grads, 0), ungroup(bias_grads, 2)
    hat_one, scale_one = norm_parts(inputs_low.astype(f32))
    first_gain_grad = jnp.sum(normed_one_grad * hat_one, (0, 1))
    first_shift_grad = jnp.sum(normed_one_grad, (0, 1))
    input_grad = (
        hidden_grad + norm_grad(normed_one_grad, hat_one, scale_one, first_gain)
    ).astype(bf16)
    small_grads = [
        first_gain_grad,
        first_shift_grad,
        query_bias_grad,
        value_bias_grad,
        out_bias_grad,
        second_gain_grad,
        second_shift_grad,
        down_bias_grad,
        up_bias_grad,
    ]
    input_grad, small_grads = flow.point(
        (input_grad, small_grads), "down", "up", "out", "a", "b"
    )
    input_grad = images_to_tokens(input_grad, member, group)
    count = lax.axis_size("fsdp")
    packed = jnp.concatenate([v.reshape(count, -1) for v in small_grads], 1)
    flow.start("small", sum_chain(packed))
    flow.point((), *flow.pending)
    flow.point((), *flow.pending)
    flow.point((), *flow.pending)
    input_grad = flow.point(input_grad, *flow.pending)
    flow.finish()
    sums = flow.results
    up_owned, down_owned, out_owned = (sums[name].astype(f32) for name in ("up", "down", "out"))
    down_owned = down_owned.T
    query_owned, key_owned, value_owned = (
        ungroup([sums["a"], sums["b"]], which).astype(f32) for which in range(3)
    )

    packed = take_block(sums["small"], shard, 1)[0]
    (
        first_gain_owned,
        first_shift_owned,
        query_bias_owned,
        value_bias_owned,
        out_bias_owned,
        second_gain_owned,
        second_shift_owned,
        down_bias_owned,
        up_bias_owned,
    ) = (packed[a:b] for a, b in zip(starts[:-1], starts[1:]))
    return (
        output,
        input_grad,
        first_gain_owned,
        first_shift_owned,
        query_owned,
        query_bias_owned,
        key_owned,
        value_owned,
        value_bias_owned,
        out_owned,
        out_bias_owned,
        second_gain_owned,
        second_shift_owned,
        up_owned,
        up_bias_owned,
        down_owned,
        down_bias_owned,
    )


def solution(mesh):
    tokens, vector, matrix = P("fsdp", "seq", None), P("fsdp"), P("fsdp", None)
    in_specs = (
        tokens,
        matrix,
        vector,
        vector,
        matrix,
        vector,
        matrix,
        matrix,
        vector,
        matrix,
        vector,
        vector,
        vector,
        matrix,
        vector,
        P(None, "fsdp"),
        vector,
        tokens,
    )
    out_specs = (
        tokens,
        tokens,
        vector,
        vector,
        matrix,
        vector,
        matrix,
        matrix,
        vector,
        matrix,
        vector,
        vector,
        vector,
        matrix,
        vector,
        P(None, "fsdp"),
        vector,
    )
    return jax.shard_map(body, mesh=mesh, in_specs=in_specs, out_specs=out_specs, check_vma=False)
```

```python
import math

import jax
import jax.numpy as jnp
from jax import lax
from jax.experimental import pallas as pl
from jax.experimental.layout import Layout, with_layout_constraint
from jax.experimental.pallas import tpu as pltpu
from jax.sharding import PartitionSpec as P

HD = 72
SEQ = 736
EPS = 1e-06
SCALE = 1.0 / math.sqrt(HD)
SCALE_LOG2 = SCALE * math.log2(math.e)
HEAD_GROUPS = ((0, 8), (8, 8))
STEP_HEADS = 4

GELU_A = math.sqrt(2 / math.pi)
GELU_B = 0.044715 * GELU_A

f32 = jnp.float32
bf16 = jnp.bfloat16


def dot2(a, b, ca, cb):
    return lax.dot_general(a, b, (((ca,), (cb,)), ((), ())), preferred_element_type=f32)


def split3(v):
    high = v.astype(bf16).astype(f32)
    mid = (v - high).astype(bf16).astype(f32)
    return [high, mid, v - high - mid]


def rows8(rows, length):
    row = lax.broadcasted_iota(jnp.int32, (8, length), 0)
    out = jnp.zeros((8, length), f32)
    for j, value in enumerate(rows):
        out = jnp.where(row == j, value, out)
    return out


def attend_forward_kernel(q_ref, k_ref, v_ref, mask_ref, context_ref, lse_ref):
    length = q_ref.shape[-1]
    bias = jnp.where(mask_ref[0] > 0, 0.0, -1e30).astype(f32)
    key_rows = rows8([bias], length)
    query_rows = rows8([jnp.ones((1, length), f32)], length)
    zeros = jnp.zeros((8, length), f32)
    ones = jnp.ones((8, length), f32)
    for h in range(STEP_HEADS):
        rows = slice(h * HD, (h + 1) * HD)
        keys = k_ref[0, rows].astype(f32)
        key_side = jnp.concatenate([keys, key_rows, keys, zeros], 0).T.astype(bf16)
        scaled = q_ref[0, rows].astype(f32) * SCALE_LOG2
        high = scaled.astype(bf16).astype(f32)
        query_side = jnp.concatenate([high, query_rows, scaled - high, zeros], 0).astype(bf16)
        value_side = jnp.concatenate([v_ref[0, rows].astype(f32), ones], 0).astype(bf16)
        scores = dot2(key_side, query_side, 1, 0)
        top = jnp.max(scores, 0, keepdims=True)
        probs = jnp.exp2(scores - top).astype(bf16)
        summed = dot2(value_side, probs, 1, 0)
        total = summed[HD : HD + 1]
        context_ref[0, rows] = (summed[:HD] * (1.0 / total)).astype(bf16)
        lse_ref[0, h] = top + jnp.log2(total)


def attend_forward(projected, mask):
    images, features, length = projected.shape
    width = features // 3
    heads = width // HD
    steps = heads // STEP_HEADS
    rows = STEP_HEADS * HD
    sources = [
        pl.BlockSpec((1, rows, length), lambda i, h, which=which: (i, which * steps + h, 0))
        for which in range(3)
    ]
    return pl.pallas_call(
        attend_forward_kernel,
        grid=(images, steps),
        in_specs=sources + [pl.BlockSpec((1, 1, length), lambda i, h: (i, 0, 0))],
        out_specs=[
            pl.BlockSpec((1, rows, length), lambda i, h: (i, h, 0)),
            pl.BlockSpec((1, STEP_HEADS, 1, length), lambda i, h: (i, h, 0, 0)),
        ],
        out_shape=[
            jax.ShapeDtypeStruct((images, width, length), bf16),
            jax.ShapeDtypeStruct((images, heads, 1, length), f32),
        ],
        compiler_params=pltpu.CompilerParams(vmem_limit_bytes=50 << 20),
        cost_estimate=pl.CostEstimate(
            flops=images * heads * length * length * 1024,
            bytes_accessed=images * width * length * 8,
            transcendentals=images * heads * length * length,
        ),
        name="attend_forward",
    )(projected, projected, projected, mask)


def attend_backward_kernel(
    q_ref, k_ref, v_ref, context_ref, grad_ref, lse_ref, mask_ref, *rest
):
    all_ref, out_ref = rest[-2:]
    length = q_ref.shape[-1]
    bias = jnp.where(mask_ref[0] > 0, 0.0, -1e30).astype(f32)
    one = jnp.ones((1, length), f32)
    key_rows = rows8([bias, one, one, one], length)
    value_rows = rows8([one, one, one], length)
    zeros = jnp.zeros((8, length), f32)
    for h in range(STEP_HEADS):
        rows = slice(h * HD, (h + 1) * HD)
        key_low = k_ref[0, rows]
        keys = key_low.astype(f32)
        key_side = jnp.concatenate([keys, key_rows, keys, zeros], 0).T.astype(bf16)
        queries = q_ref[0, rows].astype(f32)
        scaled = queries * SCALE_LOG2
        high = scaled.astype(bf16).astype(f32)
        query_side = jnp.concatenate(
            [high, rows8([one] + split3(-lse_ref[0, h]), length), scaled - high, zeros], 0
        ).astype(bf16)
        grads = grad_ref[0, rows].astype(f32)
        row_dot = jnp.sum(grads * context_ref[0, rows].astype(f32), 0, keepdims=True)
        grad_side = jnp.concatenate([grads, rows8(split3(-row_dot), length)], 0).astype(bf16)
        value_side = jnp.concatenate([v_ref[0, rows].astype(f32), value_rows], 0).T.astype(bf16)
        probs = jnp.exp2(dot2(key_side, query_side, 1, 0))
        score_grads = (probs * dot2(value_side, grad_side, 1, 0)).astype(bf16)
        dq = dot2(key_low, score_grads, 1, 0) * SCALE
        dk = (dot2(score_grads, queries.T.astype(bf16), 1, 0) * SCALE).T
        dv = dot2(probs.astype(bf16), grads.T.astype(bf16), 1, 0).T
        for which, value in enumerate((dq, dk, dv)):
            out_ref[0, which, rows] = value.astype(bf16)
            all_ref[0, which, rows] = value.astype(bf16)


def attend_backward(projected, context, grads, lse, mask, step, group, held_all, held_part):
    images, features, length = projected.shape
    heads = features // (3 * HD)
    steps = heads // STEP_HEADS
    rows = STEP_HEADS * HD
    first, count = (v // STEP_HEADS for v in group)
    block = pl.BlockSpec((1, rows, length), lambda i: (i, step, 0))
    sources = [
        pl.BlockSpec((1, rows, length), lambda i, which=which: (i, which * steps + step, 0))
        for which in range(3)
    ]
    held = [v for v in (held_all, held_part) if v is not None]
    aliases = {7 + k: k for k in range(len(held))}
    return pl.pallas_call(
        attend_backward_kernel,
        grid=(images,),
        in_specs=sources
        + [
            block,
            block,
            pl.BlockSpec((1, STEP_HEADS, 1, length), lambda i: (i, step, 0, 0)),
            pl.BlockSpec((1, 1, length), lambda i: (i, 0, 0)),
        ]
        + [pl.BlockSpec(memory_space=pl.ANY)] * len(held),
        out_specs=[
            pl.BlockSpec((1, 3, rows, length), lambda i: (i, 0, step, 0)),
            pl.BlockSpec((1, 3, rows, length), lambda i: (i, 0, step - first, 0)),
        ],
        out_shape=[
            jax.ShapeDtypeStruct((images, 3, n * rows, length), bf16) for n in (steps, count)
        ],
        input_output_aliases=aliases,
        compiler_params=pltpu.CompilerParams(vmem_limit_bytes=50 << 20),
        cost_estimate=pl.CostEstimate(
            flops=images * STEP_HEADS * length * length * 25600,
            bytes_accessed=images * rows * length * 22,
            transcendentals=images * STEP_HEADS * length * length,
        ),
        name="attend_backward",
    )(projected, projected, projected, context, grads, lse, mask, *held)


def swap(values, axis, bits):
    return lax.ppermute(values, axis, [(i, i ^ bits) for i in range(lax.axis_size(axis))])


def take_block(values, index, size):
    return lax.dynamic_slice_in_dim(values, index * size, size, 0)


def exchange(blocks):
    group, count = blocks.shape[0], lax.axis_size("seq")
    groups = [list(range(k, k + group)) for k in range(0, count, group)]
    return lax.all_to_all(blocks, "seq", 0, 0, axis_index_groups=groups)


def tokens_to_images(tokens, group):
    rows, local, width = tokens.shape
    blocks = exchange(tokens.reshape(group, rows // group, local, width))
    return jnp.swapaxes(blocks, 0, 1).reshape(rows // group, group * local, width)


def images_to_tokens(images, group):
    share, length, width = images.shape
    blocks = jnp.swapaxes(images.reshape(share, group, length // group, width), 0, 1)
    return exchange(blocks).reshape(share * group, length // group, width)


def gather_small(local):
    me = lax.axis_index("fsdp")
    count = lax.axis_size("fsdp")
    held = local[None]
    bit = 1
    while bit < count:
        held = jnp.concatenate([held, swap(held, "fsdp", bit)], 0)
        bit *= 2
    return jnp.concatenate([take_block(held, me ^ j, 1) for j in range(count)], 0)


def sum_chain(values, group):
    for axis, step in (("fsdp", 1), ("seq", 1), ("seq", group)):
        count = lax.axis_size(axis)
        reach = count if axis == "fsdp" else group if step == 1 else count // group
        if reach > 1:
            flight = yield [values] + [swap(values, axis, step * j) for j in range(1, reach)]
            values = sum(flight[1:], flight[0])
    return values


def in_order(pieces, member):
    bit = 1
    while bit < len(pieces):
        here = (member // bit) % 2
        pieces = [
            jnp.where(here == 0, piece, pieces[k ^ bit]) for k, piece in enumerate(pieces)
        ]
        bit *= 2
    return jnp.concatenate(pieces, 0)


def rows_first(values):
    return with_layout_constraint(values, Layout((0, 1)))


def sum_pieces(wholes, group, member, piece):
    flight = yield [
        [swap(take_block(whole, member ^ j, piece), "seq", j) if j else whole for j in range(group)]
        for whole in wholes
    ]
    return [
        sum((v.astype(f32) for v in came), take_block(whole, member, piece).astype(f32)).astype(bf16)
        for whole, *came in flight
    ]


def reduce_chain(fulls, group, calls=()):
    wholes = yield [
        lax.psum_scatter(full, "fsdp", scatter_dimension=0, tiled=True) for full in fulls
    ]
    member = lax.axis_index("seq") % group
    piece = wholes[0].shape[0] // group
    if 1 in calls:
        flight = yield [exchange(whole.reshape(group, piece, -1)) for whole in wholes]
        parts = [jnp.sum(came.astype(f32), 0).astype(bf16) for came in flight]
    else:
        parts = yield from sum_pieces(wholes, group, member, piece)
    bit = group
    while bit < lax.axis_size("seq"):
        if 2 in calls:
            pairs = [[i, i ^ bit] for i in range(lax.axis_size("seq")) if not i & bit]
            flight = yield [
                lax.all_to_all(
                    jnp.broadcast_to(part, (2, *part.shape)), "seq", 0, 0, axis_index_groups=pairs
                )
                for part in parts
            ]
        else:
            flight = yield [(part, swap(part, "seq", bit)) for part in parts]
        parts = [(came[0].astype(f32) + came[1].astype(f32)).astype(bf16) for came in flight]
        bit *= 2
    if 3 in calls:
        flight = yield [exchange(jnp.broadcast_to(part, (group, *part.shape))) for part in parts]
        return [came.reshape(group * piece, -1).astype(f32) for came in flight]
    flight = yield [
        [swap(part, "seq", j) if j else part for j in range(group)] for part in parts
    ]
    return [in_order(pieces, member).astype(f32) for pieces in flight]


def gather_chain(weight):
    if lax.axis_size("fsdp") != 4:
        return (yield lax.all_gather(weight, "fsdp", axis=0, tiled=True))
    sibling, far = yield (swap(weight, "fsdp", 1), swap(weight, "fsdp", 2))
    (far_sibling,) = yield (swap(far, "fsdp", 1),)
    return rows_first(in_order([weight, sibling, far, far_sibling], lax.axis_index("fsdp")))


class Flow:
    def __init__(self):
        self.chains, self.pending, self.results = {}, {}, {}

    def start(self, name, chain):
        self.chains[name], self.pending[name] = chain, next(chain)

    def point(self, main, *names):
        names = [name for name in names if name in self.pending]
        main, ended = lax.optimization_barrier((main, [self.pending[n] for n in names]))
        for name, values in zip(names, ended):
            self.advance(name, values)
        return main

    def hold(self, main, *names):
        main, ended = lax.optimization_barrier((main, [self.pending[n] for n in names]))
        self.pending.update(zip(names, ended))
        return main

    def advance(self, name, values):
        try:
            self.pending[name] = self.chains[name].send(values)
        except StopIteration as end:
            self.results[name] = end.value
            del self.pending[name]

    def finish(self):
        while self.pending:
            self.point((), *self.pending)


def ungroup(parts, which):
    return jnp.concatenate(
        [
            part[..., which * heads * HD : (which + 1) * heads * HD]
            for part, (_, heads) in zip(parts, HEAD_GROUPS)
        ],
        -1,
    )


def norm_parts(values):
    center = values - jnp.mean(values, -1, keepdims=True)
    spread = jnp.mean(center * center, -1, keepdims=True)
    scale = lax.rsqrt(spread + EPS)
    return center * scale, scale


def norm_grad(grad, hat, scale, gain):
    e = grad * gain
    return scale * (
        e - jnp.mean(e, -1, keepdims=True) - hat * jnp.mean(e * hat, -1, keepdims=True)
    )


def ein(spec, a, b):
    return jnp.einsum(spec, a, b, preferred_element_type=f32)


def token_sum(values):
    return jnp.sum(values.astype(f32), (0, 1))


def body(
    patches,
    key_mask,
    attn_norm_gain,
    attn_norm_bias,
    query_weight,
    query_bias,
    key_weight,
    value_weight,
    value_bias,
    out_weight,
    out_bias,
    mlp_norm_gain,
    mlp_norm_bias,
    up_weight,
    up_bias,
    down_weight,
    down_bias,
    cotangent,
):
    rows, local, width = patches.shape
    group = SEQ // local
    share = rows // group
    shard = lax.axis_index("fsdp")
    seq = lax.axis_index("seq")
    member = seq % group

    flow = Flow()
    inputs_low = tokens_to_images(patches, group)

    small = [
        attn_norm_gain,
        attn_norm_bias,
        query_bias,
        value_bias,
        out_bias,
        mlp_norm_gain,
        mlp_norm_bias,
        down_bias,
        up_bias,
    ]
    gathered = gather_small(jnp.concatenate(small)).astype(f32)
    starts = [0]
    for v in small:
        starts.append(starts[-1] + v.shape[0])
    (
        first_gain,
        first_shift,
        query_shift,
        value_shift,
        out_shift,
        second_gain,
        second_shift,
        down_shift,
        up_shift,
    ) = (gathered[:, a:b].reshape(-1) for a, b in zip(starts[:-1], starts[1:]))

    def whole(weight):
        return lax.all_gather(weight, "fsdp", axis=0, tiled=True)

    project_full = whole(jnp.concatenate([query_weight, key_weight, value_weight], 1))
    project_shift = jnp.concatenate([query_shift, jnp.zeros_like(query_shift), value_shift])
    inputs_low, out_local = lax.optimization_barrier((inputs_low, out_weight))
    flow.start("out_weight", gather_chain(out_local))
    up_full = whole(up_weight)
    down_full = whole(down_weight.T)

    image_mask = lax.dynamic_slice(
        key_mask, (member * share, (seq // group) * SEQ), (share, SEQ)
    )
    key_keep = image_mask[:, None, :]

    inputs = inputs_low.astype(f32)
    hat_one, _ = norm_parts(inputs)
    normed_one = (hat_one * first_gain + first_shift).astype(bf16)
    projected = (ein("itd,dm->imt", normed_one, project_full) + project_shift[:, None]).astype(
        bf16
    )
    projected, cotangent = flow.point((projected, cotangent), "out_weight")
    cotangent_low = tokens_to_images(cotangent, group)
    context, lse = attend_forward(projected, key_keep)
    if "out_weight" in flow.pending:
        context, lse = flow.point((context, lse), "out_weight")
    out_full = flow.results["out_weight"]
    hidden = inputs + ein("int,nd->itd", context, out_full) + out_shift
    hat_two, scale_two = norm_parts(hidden)
    normed_two = (hat_two * second_gain + second_shift).astype(bf16)
    pre = ein("itd,df->itf", normed_two, up_full) + up_shift
    square = pre * pre
    tanh = jnp.tanh(pre * (GELU_A + GELU_B * square))
    half_pre = 0.5 * pre
    active, slope = lax.optimization_barrier(
        (
            (half_pre + half_pre * tanh).astype(bf16),
            (
                0.5 + 0.5 * tanh + half_pre * (1.0 - tanh * tanh) * (GELU_A + 3 * GELU_B * square)
            ).astype(bf16),
        )
    )
    out_grad_low = jnp.where(image_mask[:, :, None] > 0, cotangent_low, 0).astype(bf16)
    down_grad = rows_first(ein("itd,itf->df", out_grad_low, active).astype(bf16))
    down_bias_grad = token_sum(out_grad_low)
    active, slope, out_grad_low, down_grad = flow.point((active, slope, out_grad_low, down_grad))
    flow.start("down", reduce_chain([down_grad], group, (1,)))
    output = (hidden + ein("itf,df->itd", active, down_full) + down_shift).astype(bf16)
    output, slope = flow.point((output, slope))
    output = images_to_tokens(output, group)
    pre_grad = (ein("itd,df->itf", out_grad_low, down_full) * slope.astype(f32)).astype(bf16)
    up_bias_grad = token_sum(pre_grad)
    up_grad = rows_first(ein("itd,itf->df", normed_two, pre_grad).astype(bf16))
    pre_grad, up_grad, output = flow.point((pre_grad, up_grad, output))
    flow.start("up", reduce_chain([up_grad], group, (1, 2, 3)))
    normed_two_grad = ein("itf,df->itd", pre_grad, up_full)
    hidden_grad = out_grad_low.astype(f32) + norm_grad(
        normed_two_grad, hat_two, scale_two, second_gain
    )
    second_gain_grad = jnp.sum(normed_two_grad * hat_two, (0, 1))
    second_shift_grad = jnp.sum(normed_two_grad, (0, 1))
    hidden_grad, output = flow.point((hidden_grad, output), "down")

    attn_grad_low = hidden_grad.astype(bf16)
    context_grad = ein("nd,itd->int", out_full, attn_grad_low).astype(bf16)
    out_grad = rows_first(ein("int,itd->nd", context, attn_grad_low).astype(bf16))
    out_bias_grad = token_sum(attn_grad_low)
    context_grad, out_grad = flow.point((context_grad, out_grad), "down")
    grads, parts = None, []
    per_group = HEAD_GROUPS[0][1] // STEP_HEADS
    points = ((), ("down", "up"), ("up",), ("up",))
    for step in range(len(HEAD_GROUPS) * per_group):
        number, inside = divmod(step, per_group)
        grads, part = attend_backward(
            projected,
            context,
            context_grad,
            lse,
            key_keep,
            step,
            HEAD_GROUPS[number],
            grads,
            part if inside else None,
        )
        grads, part, context_grad = flow.point((grads, part, context_grad), *points[step])
        if inside == per_group - 1:
            part = part.reshape(part.shape[0], -1, SEQ)
            parts.append(part)
            weight_grad = rows_first(ein("itd,imt->dm", normed_one, part).astype(bf16))
            grads, weight_grad, context_grad = flow.point(
                (grads, weight_grad, context_grad), *(["out_a"] if number else [])
            )
            if number:
                flow.start("b", reduce_chain([weight_grad], group))
            else:
                flow.start("out_a", reduce_chain([out_grad, weight_grad], group))
    bias_grads = [jnp.sum(part.astype(f32), (0, 2)) for part in parts]
    normed_one_grad = ein("imt,dm->itd", grads.reshape(projected.shape), project_full)
    query_bias_grad, value_bias_grad = ungroup(bias_grads, 0), ungroup(bias_grads, 2)
    hat_one, scale_one = norm_parts(inputs_low.astype(f32))
    first_gain_grad = jnp.sum(normed_one_grad * hat_one, (0, 1))
    first_shift_grad = jnp.sum(normed_one_grad, (0, 1))
    input_grad = (
        hidden_grad + norm_grad(normed_one_grad, hat_one, scale_one, first_gain)
    ).astype(bf16)
    small_grads = [
        first_gain_grad,
        first_shift_grad,
        query_bias_grad,
        value_bias_grad,
        out_bias_grad,
        second_gain_grad,
        second_shift_grad,
        down_bias_grad,
        up_bias_grad,
    ]
    input_grad, small_grads = flow.point(
        (input_grad, small_grads), "down", "up", "out_a", "b"
    )
    input_grad = images_to_tokens(input_grad, group)
    count = lax.axis_size("fsdp")
    packed = jnp.concatenate([v.reshape(count, -1) for v in small_grads], 1)
    flow.start("small", sum_chain(packed, group))
    flow.point((), "out_a", "b", "small")
    input_grad = flow.point(input_grad, *flow.pending)
    flow.finish()
    sums = flow.results
    (up_owned,), (down_owned,), (out_owned, part_a), (part_b,) = (
        sums[name] for name in ("up", "down", "out_a", "b")
    )
    down_owned = down_owned.T
    query_owned, key_owned, value_owned = (
        ungroup([part_a, part_b], which) for which in range(3)
    )

    packed = take_block(sums["small"], shard, 1)[0]
    (
        first_gain_owned,
        first_shift_owned,
        query_bias_owned,
        value_bias_owned,
        out_bias_owned,
        second_gain_owned,
        second_shift_owned,
        down_bias_owned,
        up_bias_owned,
    ) = (packed[a:b] for a, b in zip(starts[:-1], starts[1:]))
    return (
        output,
        input_grad,
        first_gain_owned,
        first_shift_owned,
        query_owned,
        query_bias_owned,
        key_owned,
        value_owned,
        value_bias_owned,
        out_owned,
        out_bias_owned,
        second_gain_owned,
        second_shift_owned,
        up_owned,
        up_bias_owned,
        down_owned,
        down_bias_owned,
    )


def solution(mesh):
    tokens, vector, matrix = P("fsdp", "seq", None), P("fsdp"), P("fsdp", None)
    in_specs = (
        tokens,
        matrix,
        vector,
        vector,
        matrix,
        vector,
        matrix,
        matrix,
        vector,
        matrix,
        vector,
        vector,
        vector,
        matrix,
        vector,
        P(None, "fsdp"),
        vector,
        tokens,
    )
    out_specs = (
        tokens,
        tokens,
        vector,
        vector,
        matrix,
        vector,
        matrix,
        matrix,
        vector,
        matrix,
        vector,
        vector,
        vector,
        matrix,
        vector,
        P(None, "fsdp"),
        vector,
    )
    return jax.shard_map(body, mesh=mesh, in_specs=in_specs, out_specs=out_specs, check_vma=False)
```

```python
import math

import jax
import jax.numpy as jnp
from jax import lax
from jax.experimental import pallas as pl
from jax.experimental.layout import Layout, with_layout_constraint
from jax.experimental.pallas import tpu as pltpu
from jax.sharding import PartitionSpec as P

HD = 72
SEQ = 736
EPS = 1e-06
SCALE = 1.0 / math.sqrt(HD)
SCALE_LOG2 = SCALE * math.log2(math.e)
HEAD_GROUPS = ((0, 8), (8, 8))
STEP_HEADS = 4

GELU_A = math.sqrt(2 / math.pi)
GELU_B = 0.044715 * GELU_A

f32 = jnp.float32
bf16 = jnp.bfloat16


def dot2(a, b, ca, cb):
    return lax.dot_general(a, b, (((ca,), (cb,)), ((), ())), preferred_element_type=f32)


def split3(v):
    high = v.astype(bf16).astype(f32)
    mid = (v - high).astype(bf16).astype(f32)
    return [high, mid, v - high - mid]


def rows8(rows, length):
    row = lax.broadcasted_iota(jnp.int32, (8, length), 0)
    out = jnp.zeros((8, length), f32)
    for j, value in enumerate(rows):
        out = jnp.where(row == j, value, out)
    return out


def attend_forward_kernel(q_ref, k_ref, v_ref, mask_ref, context_ref, lse_ref):
    length = q_ref.shape[-1]
    bias = jnp.where(mask_ref[0] > 0, 0.0, -1e30).astype(f32)
    key_rows = rows8([bias], length)
    query_rows = rows8([jnp.ones((1, length), f32)], length)
    zeros = jnp.zeros((8, length), f32)
    ones = jnp.ones((8, length), f32)
    for h in range(STEP_HEADS):
        rows = slice(h * HD, (h + 1) * HD)
        keys = k_ref[0, rows].astype(f32)
        key_side = jnp.concatenate([keys, key_rows, keys, zeros], 0).T.astype(bf16)
        scaled = q_ref[0, rows].astype(f32) * SCALE_LOG2
        high = scaled.astype(bf16).astype(f32)
        query_side = jnp.concatenate([high, query_rows, scaled - high, zeros], 0).astype(bf16)
        value_side = jnp.concatenate([v_ref[0, rows].astype(f32), ones], 0).astype(bf16)
        scores = dot2(key_side, query_side, 1, 0)
        top = jnp.max(scores, 0, keepdims=True)
        probs = jnp.exp2(scores - top).astype(bf16)
        summed = dot2(value_side, probs, 1, 0)
        total = summed[HD : HD + 1]
        context_ref[0, rows] = (summed[:HD] * (1.0 / total)).astype(bf16)
        lse_ref[0, h] = top + jnp.log2(total)


def attend_forward(projected, mask):
    images, features, length = projected.shape
    width = features // 3
    heads = width // HD
    steps = heads // STEP_HEADS
    rows = STEP_HEADS * HD
    sources = [
        pl.BlockSpec((1, rows, length), lambda i, h, which=which: (i, which * steps + h, 0))
        for which in range(3)
    ]
    return pl.pallas_call(
        attend_forward_kernel,
        grid=(images, steps),
        in_specs=sources + [pl.BlockSpec((1, 1, length), lambda i, h: (i, 0, 0))],
        out_specs=[
            pl.BlockSpec((1, rows, length), lambda i, h: (i, h, 0)),
            pl.BlockSpec((1, STEP_HEADS, 1, length), lambda i, h: (i, h, 0, 0)),
        ],
        out_shape=[
            jax.ShapeDtypeStruct((images, width, length), bf16),
            jax.ShapeDtypeStruct((images, heads, 1, length), f32),
        ],
        compiler_params=pltpu.CompilerParams(vmem_limit_bytes=50 << 20),
        cost_estimate=pl.CostEstimate(
            flops=images * heads * length * length * 1024,
            bytes_accessed=images * width * length * 8,
            transcendentals=images * heads * length * length,
        ),
        name="attend_forward",
    )(projected, projected, projected, mask)


def attend_backward_kernel(
    q_ref, k_ref, v_ref, context_ref, grad_ref, lse_ref, mask_ref, *rest
):
    all_ref, out_ref = rest[-2:]
    length = q_ref.shape[-1]
    bias = jnp.where(mask_ref[0] > 0, 0.0, -1e30).astype(f32)
    one = jnp.ones((1, length), f32)
    key_rows = rows8([bias, one, one, one], length)
    value_rows = rows8([one, one, one], length)
    zeros = jnp.zeros((8, length), f32)
    for h in range(STEP_HEADS):
        rows = slice(h * HD, (h + 1) * HD)
        key_low = k_ref[0, rows]
        keys = key_low.astype(f32)
        key_side = jnp.concatenate([keys, key_rows, keys, zeros], 0).T.astype(bf16)
        queries = q_ref[0, rows].astype(f32)
        scaled = queries * SCALE_LOG2
        high = scaled.astype(bf16).astype(f32)
        query_side = jnp.concatenate(
            [high, rows8([one] + split3(-lse_ref[0, h]), length), scaled - high, zeros], 0
        ).astype(bf16)
        grads = grad_ref[0, rows].astype(f32)
        row_dot = jnp.sum(grads * context_ref[0, rows].astype(f32), 0, keepdims=True)
        grad_side = jnp.concatenate([grads, rows8(split3(-row_dot), length)], 0).astype(bf16)
        value_side = jnp.concatenate([v_ref[0, rows].astype(f32), value_rows], 0).T.astype(bf16)
        probs = jnp.exp2(dot2(key_side, query_side, 1, 0))
        score_grads = (probs * dot2(value_side, grad_side, 1, 0)).astype(bf16)
        dq = dot2(key_low, score_grads, 1, 0) * SCALE
        dk = (dot2(score_grads, queries.T.astype(bf16), 1, 0) * SCALE).T
        dv = dot2(probs.astype(bf16), grads.T.astype(bf16), 1, 0).T
        for which, value in enumerate((dq, dk, dv)):
            out_ref[0, which, rows] = value.astype(bf16)
            all_ref[0, which, rows] = value.astype(bf16)


def attend_backward(projected, context, grads, lse, mask, step, group, held_all, held_part):
    images, features, length = projected.shape
    heads = features // (3 * HD)
    steps = heads // STEP_HEADS
    rows = STEP_HEADS * HD
    first, count = (v // STEP_HEADS for v in group)
    block = pl.BlockSpec((1, rows, length), lambda i: (i, step, 0))
    sources = [
        pl.BlockSpec((1, rows, length), lambda i, which=which: (i, which * steps + step, 0))
        for which in range(3)
    ]
    held = [v for v in (held_all, held_part) if v is not None]
    aliases = {7 + k: k for k in range(len(held))}
    return pl.pallas_call(
        attend_backward_kernel,
        grid=(images,),
        in_specs=sources
        + [
            block,
            block,
            pl.BlockSpec((1, STEP_HEADS, 1, length), lambda i: (i, step, 0, 0)),
            pl.BlockSpec((1, 1, length), lambda i: (i, 0, 0)),
        ]
        + [pl.BlockSpec(memory_space=pl.ANY)] * len(held),
        out_specs=[
            pl.BlockSpec((1, 3, rows, length), lambda i: (i, 0, step, 0)),
            pl.BlockSpec((1, 3, rows, length), lambda i: (i, 0, step - first, 0)),
        ],
        out_shape=[
            jax.ShapeDtypeStruct((images, 3, n * rows, length), bf16) for n in (steps, count)
        ],
        input_output_aliases=aliases,
        compiler_params=pltpu.CompilerParams(vmem_limit_bytes=50 << 20),
        cost_estimate=pl.CostEstimate(
            flops=images * STEP_HEADS * length * length * (256 if step == steps - 1 else 25600),
            bytes_accessed=images * rows * length * (1 if step == steps - 1 else 22),
            transcendentals=images * length,
        ),
        name="attend_backward",
    )(projected, projected, projected, context, grads, lse, mask, *held)


def swap(values, axis, bits):
    return lax.ppermute(values, axis, [(i, i ^ bits) for i in range(lax.axis_size(axis))])


def take_block(values, index, size):
    return lax.dynamic_slice_in_dim(values, index * size, size, 0)


def exchange(blocks):
    group, count = blocks.shape[0], lax.axis_size("seq")
    groups = [list(range(k, k + group)) for k in range(0, count, group)]
    return lax.all_to_all(blocks, "seq", 0, 0, axis_index_groups=groups)


def tokens_to_images(tokens, group):
    rows, local, width = tokens.shape
    blocks = exchange(tokens.reshape(group, rows // group, local, width))
    return jnp.swapaxes(blocks, 0, 1).reshape(rows // group, group * local, width)


def images_to_tokens(images, group):
    share, length, width = images.shape
    blocks = jnp.swapaxes(images.reshape(share, group, length // group, width), 0, 1)
    return exchange(blocks).reshape(share * group, length // group, width)


def gather_small(local):
    me = lax.axis_index("fsdp")
    count = lax.axis_size("fsdp")
    held = local[None]
    bit = 1
    while bit < count:
        held = jnp.concatenate([held, swap(held, "fsdp", bit)], 0)
        bit *= 2
    return jnp.concatenate([take_block(held, me ^ j, 1) for j in range(count)], 0)


def sum_chain(values, group):
    for axis, step in (("fsdp", 1), ("seq", 1), ("seq", group)):
        count = lax.axis_size(axis)
        reach = count if axis == "fsdp" else group if step == 1 else count // group
        if reach > 1:
            flight = yield [values] + [swap(values, axis, step * j) for j in range(1, reach)]
            values = sum(flight[1:], flight[0])
    return values


def in_order(pieces, member):
    bit = 1
    while bit < len(pieces):
        here = (member // bit) % 2
        pieces = [
            jnp.where(here == 0, piece, pieces[k ^ bit]) for k, piece in enumerate(pieces)
        ]
        bit *= 2
    return jnp.concatenate(pieces, 0)


def rows_first(values):
    return with_layout_constraint(values, Layout((0, 1)))


def split_columns(total, widths):
    ends = [sum(widths[:k]) for k in range(len(widths) + 1)]
    return [total[:, a:b].astype(f32) for a, b in zip(ends[:-1], ends[1:])]


def sum_pieces(wholes, group, member, piece):
    flight = yield [
        [swap(take_block(whole, member ^ j, piece), "seq", j) if j else whole for j in range(group)]
        for whole in wholes
    ]
    return [
        sum((v.astype(f32) for v in came), take_block(whole, member, piece).astype(f32)).astype(bf16)
        for whole, *came in flight
    ]


def reduce_chain(fulls, group, calls=()):
    wholes = yield [
        lax.psum_scatter(full, "fsdp", scatter_dimension=0, tiled=True) for full in fulls
    ]
    widths = [whole.shape[1] for whole in wholes]
    wholes = [jnp.concatenate(wholes, 1)]
    member = lax.axis_index("seq") % group
    piece = wholes[0].shape[0] // group
    if 1 in calls:
        flight = yield [exchange(whole.reshape(group, piece, -1)) for whole in wholes]
        parts = [jnp.sum(came.astype(f32), 0).astype(bf16) for came in flight]
    else:
        parts = yield from sum_pieces(wholes, group, member, piece)
    bit = group
    while bit < lax.axis_size("seq"):
        if 2 in calls:
            pairs = [[i, i ^ bit] for i in range(lax.axis_size("seq")) if not i & bit]
            flight = yield [
                lax.all_to_all(
                    jnp.broadcast_to(part, (2, *part.shape)), "seq", 0, 0, axis_index_groups=pairs
                )
                for part in parts
            ]
        else:
            flight = yield [(part, swap(part, "seq", bit)) for part in parts]
        parts = [(came[0].astype(f32) + came[1].astype(f32)).astype(bf16) for came in flight]
        bit *= 2
    if 3 in calls:
        flight = yield [exchange(jnp.broadcast_to(part, (group, *part.shape))) for part in parts]
        (total,) = [came.reshape(group * piece, -1) for came in flight]
        return split_columns(total, widths)
    flight = yield [
        [swap(part, "seq", j) if j else part for j in range(group)] for part in parts
    ]
    (total,) = [in_order(pieces, member) for pieces in flight]
    return split_columns(total, widths)


def gather_chain(weight):
    if lax.axis_size("fsdp") != 4:
        return (yield lax.all_gather(weight, "fsdp", axis=0, tiled=True))
    sibling, far = yield (swap(weight, "fsdp", 1), swap(weight, "fsdp", 2))
    (far_sibling,) = yield (swap(far, "fsdp", 1),)
    return rows_first(in_order([weight, sibling, far, far_sibling], lax.axis_index("fsdp")))


class Flow:
    def __init__(self):
        self.chains, self.pending, self.results = {}, {}, {}

    def start(self, name, chain):
        self.chains[name], self.pending[name] = chain, next(chain)

    def point(self, main, *names):
        names = [name for name in names if name in self.pending]
        main, ended = lax.optimization_barrier((main, [self.pending[n] for n in names]))
        for name, values in zip(names, ended):
            self.advance(name, values)
        return main

    def hold(self, main, *names):
        main, ended = lax.optimization_barrier((main, [self.pending[n] for n in names]))
        self.pending.update(zip(names, ended))
        return main

    def advance(self, name, values):
        try:
            self.pending[name] = self.chains[name].send(values)
        except StopIteration as end:
            self.results[name] = end.value
            del self.pending[name]

    def finish(self):
        while self.pending:
            self.point((), *self.pending)


def ungroup(parts, which):
    return jnp.concatenate(
        [
            part[..., which * heads * HD : (which + 1) * heads * HD]
            for part, (_, heads) in zip(parts, HEAD_GROUPS)
        ],
        -1,
    )


def norm_parts(values):
    center = values - jnp.mean(values, -1, keepdims=True)
    spread = jnp.mean(center * center, -1, keepdims=True)
    scale = lax.rsqrt(spread + EPS)
    return center * scale, scale


def norm_grad(grad, hat, scale, gain):
    e = grad * gain
    return scale * (
        e - jnp.mean(e, -1, keepdims=True) - hat * jnp.mean(e * hat, -1, keepdims=True)
    )


def ein(spec, a, b):
    return jnp.einsum(spec, a, b, preferred_element_type=f32)


def token_sum(values):
    return jnp.sum(values.astype(f32), (0, 1))


def body(
    patches,
    key_mask,
    attn_norm_gain,
    attn_norm_bias,
    query_weight,
    query_bias,
    key_weight,
    value_weight,
    value_bias,
    out_weight,
    out_bias,
    mlp_norm_gain,
    mlp_norm_bias,
    up_weight,
    up_bias,
    down_weight,
    down_bias,
    cotangent,
):
    rows, local, width = patches.shape
    group = SEQ // local
    share = rows // group
    shard = lax.axis_index("fsdp")
    seq = lax.axis_index("seq")
    member = seq % group

    flow = Flow()
    inputs_low = tokens_to_images(patches, group)

    small = [
        attn_norm_gain,
        attn_norm_bias,
        query_bias,
        value_bias,
        out_bias,
        mlp_norm_gain,
        mlp_norm_bias,
        down_bias,
        up_bias,
    ]
    gathered = gather_small(jnp.concatenate(small)).astype(f32)
    starts = [0]
    for v in small:
        starts.append(starts[-1] + v.shape[0])
    (
        first_gain,
        first_shift,
        query_shift,
        value_shift,
        out_shift,
        second_gain,
        second_shift,
        down_shift,
        up_shift,
    ) = (gathered[:, a:b].reshape(-1) for a, b in zip(starts[:-1], starts[1:]))

    def whole(weight):
        return lax.all_gather(weight, "fsdp", axis=0, tiled=True)

    project_full = whole(jnp.concatenate([query_weight, key_weight, value_weight], 1))
    project_shift = jnp.concatenate([query_shift, jnp.zeros_like(query_shift), value_shift])
    inputs_low, out_local = lax.optimization_barrier((inputs_low, out_weight))
    flow.start("out_weight", gather_chain(out_local))
    up_full = whole(up_weight)
    down_full = whole(down_weight.T)

    image_mask = lax.dynamic_slice(
        key_mask, (member * share, (seq // group) * SEQ), (share, SEQ)
    )
    key_keep = image_mask[:, None, :]

    inputs = inputs_low.astype(f32)
    hat_one, _ = norm_parts(inputs)
    normed_one = (hat_one * first_gain + first_shift).astype(bf16)
    projected = (ein("itd,dm->imt", normed_one, project_full) + project_shift[:, None]).astype(
        bf16
    )
    projected, cotangent = flow.point((projected, cotangent), "out_weight")
    cotangent_low = tokens_to_images(cotangent, group)
    context, lse = attend_forward(projected, key_keep)
    if "out_weight" in flow.pending:
        context, lse = flow.point((context, lse), "out_weight")
    out_full = flow.results["out_weight"]
    hidden = inputs + ein("int,nd->itd", context, out_full) + out_shift
    hat_two, scale_two = norm_parts(hidden)
    normed_two = (hat_two * second_gain + second_shift).astype(bf16)
    pre = ein("itd,df->itf", normed_two, up_full) + up_shift
    square = pre * pre
    tanh = jnp.tanh(pre * (GELU_A + GELU_B * square))
    half_pre = 0.5 * pre
    active, slope = lax.optimization_barrier(
        (
            (half_pre + half_pre * tanh).astype(bf16),
            (
                0.5 + 0.5 * tanh + half_pre * (1.0 - tanh * tanh) * (GELU_A + 3 * GELU_B * square)
            ).astype(bf16),
        )
    )
    out_grad_low = jnp.where(image_mask[:, :, None] > 0, cotangent_low, 0).astype(bf16)
    down_grad = rows_first(ein("itd,itf->df", out_grad_low, active).astype(bf16))
    down_bias_grad = token_sum(out_grad_low)
    active, slope, out_grad_low, down_grad = flow.point((active, slope, out_grad_low, down_grad))
    flow.start("down", reduce_chain([down_grad], group, (1,)))
    output = (hidden + ein("itf,df->itd", active, down_full) + down_shift).astype(bf16)
    output, slope = flow.point((output, slope))
    output = images_to_tokens(output, group)
    pre_grad = (ein("itd,df->itf", out_grad_low, down_full) * slope.astype(f32)).astype(bf16)
    up_bias_grad = token_sum(pre_grad)
    up_grad = rows_first(ein("itd,itf->df", normed_two, pre_grad).astype(bf16))
    pre_grad, up_grad, output = flow.point((pre_grad, up_grad, output), "down")
    flow.start("up", reduce_chain([up_grad], group, (1, 2)))
    normed_two_grad = ein("itf,df->itd", pre_grad, up_full)
    hidden_grad = out_grad_low.astype(f32) + norm_grad(
        normed_two_grad, hat_two, scale_two, second_gain
    )
    second_gain_grad = jnp.sum(normed_two_grad * hat_two, (0, 1))
    second_shift_grad = jnp.sum(normed_two_grad, (0, 1))
    hidden_grad, output = flow.point((hidden_grad, output), "down")

    attn_grad_low = hidden_grad.astype(bf16)
    context_grad = ein("nd,itd->int", out_full, attn_grad_low).astype(bf16)
    out_grad = rows_first(ein("int,itd->nd", context, attn_grad_low).astype(bf16))
    context_grad, out_grad = flow.point((context_grad, out_grad), "down")
    grads, parts = None, []
    per_group = HEAD_GROUPS[0][1] // STEP_HEADS
    points = (("up",), (), ("down",), ("up",))
    for step in range(len(HEAD_GROUPS) * per_group):
        number, inside = divmod(step, per_group)
        grads, part = attend_backward(
            projected,
            context,
            context_grad,
            lse,
            key_keep,
            step,
            HEAD_GROUPS[number],
            grads,
            part if inside else None,
        )
        if step == 3:
            out_bias_grad = token_sum(attn_grad_low)
            bias_grads = [jnp.sum(parts[0].astype(f32), (0, 2))]
            part, out_bias_grad, bias_grads = lax.optimization_barrier(
                (part, out_bias_grad, bias_grads)
            )
        grads, part, context_grad, attn_grad_low, parts = flow.point(
            (grads, part, context_grad, attn_grad_low, parts), *points[step]
        )
        if inside == per_group - 1:
            part = part.reshape(part.shape[0], -1, SEQ)
            parts.append(part)
            weight_grad = rows_first(ein("itd,imt->dm", normed_one, part).astype(bf16))
            grads, weight_grad, context_grad = flow.point(
                (grads, weight_grad, context_grad), *(["out_a"] if number else ["up"])
            )
            if number:
                flow.start("b", reduce_chain([weight_grad], group))
            else:
                flow.start("out_a", reduce_chain([out_grad, weight_grad], group, (1,)))
    bias_grads.append(jnp.sum(parts[1].astype(f32), (0, 2)))
    normed_one_grad = ein("imt,dm->itd", grads.reshape(projected.shape), project_full)
    query_bias_grad, value_bias_grad = ungroup(bias_grads, 0), ungroup(bias_grads, 2)
    hat_one, scale_one = norm_parts(inputs_low.astype(f32))
    first_gain_grad = jnp.sum(normed_one_grad * hat_one, (0, 1))
    first_shift_grad = jnp.sum(normed_one_grad, (0, 1))
    input_grad = (
        hidden_grad + norm_grad(normed_one_grad, hat_one, scale_one, first_gain)
    ).astype(bf16)
    small_grads = [
        first_gain_grad,
        first_shift_grad,
        query_bias_grad,
        value_bias_grad,
        out_bias_grad,
        second_gain_grad,
        second_shift_grad,
        down_bias_grad,
        up_bias_grad,
    ]
    input_grad, small_grads = flow.point(
        (input_grad, small_grads), "down", "up", "out_a", "b"
    )
    input_grad = images_to_tokens(input_grad, group)
    count = lax.axis_size("fsdp")
    packed = jnp.concatenate([v.reshape(count, -1) for v in small_grads], 1)
    flow.start("small", sum_chain(packed, group))
    flow.point((), "out_a", "b", "small")
    input_grad = flow.point(input_grad, *flow.pending)
    flow.finish()
    sums = flow.results
    (up_owned,), (down_owned,), (out_owned, part_a), (part_b,) = (
        sums[name] for name in ("up", "down", "out_a", "b")
    )
    down_owned = down_owned.T
    query_owned, key_owned, value_owned = (
        ungroup([part_a, part_b], which) for which in range(3)
    )

    packed = take_block(sums["small"], shard, 1)[0]
    (
        first_gain_owned,
        first_shift_owned,
        query_bias_owned,
        value_bias_owned,
        out_bias_owned,
        second_gain_owned,
        second_shift_owned,
        down_bias_owned,
        up_bias_owned,
    ) = (packed[a:b] for a, b in zip(starts[:-1], starts[1:]))
    return (
        output,
        input_grad,
        first_gain_owned,
        first_shift_owned,
        query_owned,
        query_bias_owned,
        key_owned,
        value_owned,
        value_bias_owned,
        out_owned,
        out_bias_owned,
        second_gain_owned,
        second_shift_owned,
        up_owned,
        up_bias_owned,
        down_owned,
        down_bias_owned,
    )


def solution(mesh):
    tokens, vector, matrix = P("fsdp", "seq", None), P("fsdp"), P("fsdp", None)
    in_specs = (
        tokens,
        matrix,
        vector,
        vector,
        matrix,
        vector,
        matrix,
        matrix,
        vector,
        matrix,
        vector,
        vector,
        vector,
        matrix,
        vector,
        P(None, "fsdp"),
        vector,
        tokens,
    )
    out_specs = (
        tokens,
        tokens,
        vector,
        vector,
        matrix,
        vector,
        matrix,
        matrix,
        vector,
        matrix,
        vector,
        vector,
        vector,
        matrix,
        vector,
        P(None, "fsdp"),
        vector,
    )
    return jax.shard_map(body, mesh=mesh, in_specs=in_specs, out_specs=out_specs, check_vma=False)
```

```python
import math

import jax
import jax.numpy as jnp
from jax import lax
from jax.experimental import pallas as pl
from jax.experimental.layout import Layout, with_layout_constraint
from jax.experimental.pallas import tpu as pltpu
from jax.sharding import PartitionSpec as P

HD = 72
SEQ = 736
EPS = 1e-06
SCALE = 1.0 / math.sqrt(HD)
SCALE_LOG2 = SCALE * math.log2(math.e)
HEAD_GROUPS = ((0, 8), (8, 8))
STEP_HEADS = 4

GELU_A = math.sqrt(2 / math.pi)
GELU_B = 0.044715 * GELU_A

f32 = jnp.float32
bf16 = jnp.bfloat16


def dot2(a, b, ca, cb):
    return lax.dot_general(a, b, (((ca,), (cb,)), ((), ())), preferred_element_type=f32)


def split3(v):
    high = v.astype(bf16).astype(f32)
    mid = (v - high).astype(bf16).astype(f32)
    return [high, mid, v - high - mid]


def rows8(rows, length):
    row = lax.broadcasted_iota(jnp.int32, (8, length), 0)
    out = jnp.zeros((8, length), f32)
    for j, value in enumerate(rows):
        out = jnp.where(row == j, value, out)
    return out


def attend_forward_kernel(q_ref, k_ref, v_ref, mask_ref, context_ref, lse_ref):
    length = q_ref.shape[-1]
    bias = jnp.where(mask_ref[0] > 0, 0.0, -1e30).astype(f32)
    key_rows = rows8([bias], length)
    query_rows = rows8([jnp.ones((1, length), f32)], length)
    zeros = jnp.zeros((8, length), f32)
    ones = jnp.ones((8, length), f32)
    for h in range(STEP_HEADS):
        rows = slice(h * HD, (h + 1) * HD)
        keys = k_ref[0, rows].astype(f32)
        key_side = jnp.concatenate([keys, key_rows, keys, zeros], 0).T.astype(bf16)
        scaled = q_ref[0, rows].astype(f32) * SCALE_LOG2
        high = scaled.astype(bf16).astype(f32)
        query_side = jnp.concatenate([high, query_rows, scaled - high, zeros], 0).astype(bf16)
        value_side = jnp.concatenate([v_ref[0, rows].astype(f32), ones], 0).astype(bf16)
        scores = dot2(key_side, query_side, 1, 0)
        top = jnp.max(scores, 0, keepdims=True)
        probs = jnp.exp2(scores - top).astype(bf16)
        summed = dot2(value_side, probs, 1, 0)
        total = summed[HD : HD + 1]
        context_ref[0, rows] = (summed[:HD] * (1.0 / total)).astype(bf16)
        lse_ref[0, h] = top + jnp.log2(total)


def attend_forward(projected, mask):
    images, features, length = projected.shape
    width = features // 3
    heads = width // HD
    steps = heads // STEP_HEADS
    rows = STEP_HEADS * HD
    sources = [
        pl.BlockSpec((1, rows, length), lambda i, h, which=which: (i, which * steps + h, 0))
        for which in range(3)
    ]
    return pl.pallas_call(
        attend_forward_kernel,
        grid=(images, steps),
        in_specs=sources + [pl.BlockSpec((1, 1, length), lambda i, h: (i, 0, 0))],
        out_specs=[
            pl.BlockSpec((1, rows, length), lambda i, h: (i, h, 0)),
            pl.BlockSpec((1, STEP_HEADS, 1, length), lambda i, h: (i, h, 0, 0)),
        ],
        out_shape=[
            jax.ShapeDtypeStruct((images, width, length), bf16),
            jax.ShapeDtypeStruct((images, heads, 1, length), f32),
        ],
        compiler_params=pltpu.CompilerParams(vmem_limit_bytes=50 << 20),
        cost_estimate=pl.CostEstimate(
            flops=images * heads * length * length * 1024,
            bytes_accessed=images * width * length * 8,
            transcendentals=images * heads * length * length,
        ),
        name="attend_forward",
    )(projected, projected, projected, mask)


def attend_backward_kernel(
    q_ref, k_ref, v_ref, context_ref, grad_ref, lse_ref, mask_ref, *rest
):
    all_ref, out_ref = rest[-2:]
    length = q_ref.shape[-1]
    bias = jnp.where(mask_ref[0] > 0, 0.0, -1e30).astype(f32)
    one = jnp.ones((1, length), f32)
    key_rows = rows8([bias, one, one, one], length)
    value_rows = rows8([one, one, one], length)
    zeros = jnp.zeros((8, length), f32)
    for h in range(STEP_HEADS):
        rows = slice(h * HD, (h + 1) * HD)
        key_low = k_ref[0, rows]
        keys = key_low.astype(f32)
        key_side = jnp.concatenate([keys, key_rows, keys, zeros], 0).T.astype(bf16)
        queries = q_ref[0, rows].astype(f32)
        scaled = queries * SCALE_LOG2
        high = scaled.astype(bf16).astype(f32)
        query_side = jnp.concatenate(
            [high, rows8([one] + split3(-lse_ref[0, h]), length), scaled - high, zeros], 0
        ).astype(bf16)
        grads = grad_ref[0, rows].astype(f32)
        row_dot = jnp.sum(grads * context_ref[0, rows].astype(f32), 0, keepdims=True)
        grad_side = jnp.concatenate([grads, rows8(split3(-row_dot), length)], 0).astype(bf16)
        value_side = jnp.concatenate([v_ref[0, rows].astype(f32), value_rows], 0).T.astype(bf16)
        probs = jnp.exp2(dot2(key_side, query_side, 1, 0))
        score_grads = (probs * dot2(value_side, grad_side, 1, 0)).astype(bf16)
        dq = dot2(key_low, score_grads, 1, 0) * SCALE
        dk = (dot2(score_grads, queries.T.astype(bf16), 1, 0) * SCALE).T
        dv = dot2(probs.astype(bf16), grads.T.astype(bf16), 1, 0).T
        for which, value in enumerate((dq, dk, dv)):
            out_ref[0, which, rows] = value.astype(bf16)
            all_ref[0, which, rows] = value.astype(bf16)


def attend_backward(projected, context, grads, lse, mask, step, group, held_all, held_part):
    images, features, length = projected.shape
    heads = features // (3 * HD)
    steps = heads // STEP_HEADS
    rows = STEP_HEADS * HD
    first, count = (v // STEP_HEADS for v in group)
    block = pl.BlockSpec((1, rows, length), lambda i: (i, step, 0))
    sources = [
        pl.BlockSpec((1, rows, length), lambda i, which=which: (i, which * steps + step, 0))
        for which in range(3)
    ]
    held = [v for v in (held_all, held_part) if v is not None]
    aliases = {7 + k: k for k in range(len(held))}
    return pl.pallas_call(
        attend_backward_kernel,
        grid=(images,),
        in_specs=sources
        + [
            block,
            block,
            pl.BlockSpec((1, STEP_HEADS, 1, length), lambda i: (i, step, 0, 0)),
            pl.BlockSpec((1, 1, length), lambda i: (i, 0, 0)),
        ]
        + [pl.BlockSpec(memory_space=pl.ANY)] * len(held),
        out_specs=[
            pl.BlockSpec((1, 3, rows, length), lambda i: (i, 0, step, 0)),
            pl.BlockSpec((1, 3, rows, length), lambda i: (i, 0, step - first, 0)),
        ],
        out_shape=[
            jax.ShapeDtypeStruct((images, 3, n * rows, length), bf16) for n in (steps, count)
        ],
        input_output_aliases=aliases,
        compiler_params=pltpu.CompilerParams(vmem_limit_bytes=50 << 20),
        cost_estimate=pl.CostEstimate(
            flops=images * STEP_HEADS * length * length * (256 if step == steps - 1 else 25600),
            bytes_accessed=images * rows * length * (1 if step == steps - 1 else 22),
            transcendentals=images * length,
        ),
        name="attend_backward",
    )(projected, projected, projected, context, grads, lse, mask, *held)


def swap(values, axis, bits):
    return lax.ppermute(values, axis, [(i, i ^ bits) for i in range(lax.axis_size(axis))])


def take_block(values, index, size):
    return lax.dynamic_slice_in_dim(values, index * size, size, 0)


def exchange(blocks):
    group, count = blocks.shape[0], lax.axis_size("seq")
    groups = [list(range(k, k + group)) for k in range(0, count, group)]
    return lax.all_to_all(blocks, "seq", 0, 0, axis_index_groups=groups)


def tokens_to_images(tokens, group):
    rows, local, width = tokens.shape
    blocks = exchange(tokens.reshape(group, rows // group, local, width))
    return jnp.swapaxes(blocks, 0, 1).reshape(rows // group, group * local, width)


def images_to_tokens(images, group):
    share, length, width = images.shape
    blocks = jnp.swapaxes(images.reshape(share, group, length // group, width), 0, 1)
    return exchange(blocks).reshape(share * group, length // group, width)


def gather_small(local):
    me = lax.axis_index("fsdp")
    count = lax.axis_size("fsdp")
    held = local[None]
    bit = 1
    while bit < count:
        held = jnp.concatenate([held, swap(held, "fsdp", bit)], 0)
        bit *= 2
    return jnp.concatenate([take_block(held, me ^ j, 1) for j in range(count)], 0)


def sum_chain(values, group):
    for axis, step in (("fsdp", 1), ("seq", 1), ("seq", group)):
        count = lax.axis_size(axis)
        reach = count if axis == "fsdp" else group if step == 1 else count // group
        if reach > 1:
            flight = yield [values] + [swap(values, axis, step * j) for j in range(1, reach)]
            values = sum(flight[1:], flight[0])
    return values


def in_order(pieces, member):
    bit = 1
    while bit < len(pieces):
        here = (member // bit) % 2
        pieces = [
            jnp.where(here == 0, piece, pieces[k ^ bit]) for k, piece in enumerate(pieces)
        ]
        bit *= 2
    return jnp.concatenate(pieces, 0)


def rows_first(values):
    return with_layout_constraint(values, Layout((0, 1)))


def split_columns(total, widths):
    ends = [sum(widths[:k]) for k in range(len(widths) + 1)]
    return [total[:, a:b].astype(f32) for a, b in zip(ends[:-1], ends[1:])]


def sum_pieces(wholes, group, member, piece):
    flight = yield [
        [swap(take_block(whole, member ^ j, piece), "seq", j) if j else whole for j in range(group)]
        for whole in wholes
    ]
    return [
        sum((v.astype(f32) for v in came), take_block(whole, member, piece).astype(f32)).astype(bf16)
        for whole, *came in flight
    ]


def reduce_chain(fulls, group, calls=()):
    wholes = yield [
        lax.psum_scatter(full, "fsdp", scatter_dimension=0, tiled=True) for full in fulls
    ]
    widths = [whole.shape[1] for whole in wholes]
    wholes = [jnp.concatenate(wholes, 1)]
    member = lax.axis_index("seq") % group
    piece = wholes[0].shape[0] // group
    if 1 in calls:
        flight = yield [exchange(whole.reshape(group, piece, -1)) for whole in wholes]
        parts = [jnp.sum(came.astype(f32), 0).astype(bf16) for came in flight]
    else:
        parts = yield from sum_pieces(wholes, group, member, piece)
    bit = group
    while bit < lax.axis_size("seq"):
        if 2 in calls:
            pairs = [[i, i ^ bit] for i in range(lax.axis_size("seq")) if not i & bit]
            flight = yield [
                lax.all_to_all(
                    jnp.broadcast_to(part, (2, *part.shape)), "seq", 0, 0, axis_index_groups=pairs
                )
                for part in parts
            ]
        else:
            flight = yield [(part, swap(part, "seq", bit)) for part in parts]
        parts = [(came[0].astype(f32) + came[1].astype(f32)).astype(bf16) for came in flight]
        bit *= 2
    if 3 in calls:
        flight = yield [exchange(jnp.broadcast_to(part, (group, *part.shape))) for part in parts]
        (total,) = [came.reshape(group * piece, -1) for came in flight]
        return split_columns(total, widths)
    flight = yield [
        [swap(part, "seq", j) if j else part for j in range(group)] for part in parts
    ]
    (total,) = [in_order(pieces, member) for pieces in flight]
    return split_columns(total, widths)


def gather_chain(weight):
    if lax.axis_size("fsdp") != 4:
        return (yield lax.all_gather(weight, "fsdp", axis=0, tiled=True))
    sibling, far = yield (swap(weight, "fsdp", 1), swap(weight, "fsdp", 2))
    (far_sibling,) = yield (swap(far, "fsdp", 1),)
    return rows_first(in_order([weight, sibling, far, far_sibling], lax.axis_index("fsdp")))


class Flow:
    def __init__(self):
        self.chains, self.pending, self.results = {}, {}, {}

    def start(self, name, chain):
        self.chains[name], self.pending[name] = chain, next(chain)

    def point(self, main, *names):
        names = [name for name in names if name in self.pending]
        main, ended = lax.optimization_barrier((main, [self.pending[n] for n in names]))
        for name, values in zip(names, ended):
            self.advance(name, values)
        return main

    def hold(self, main, *names):
        main, ended = lax.optimization_barrier((main, [self.pending[n] for n in names]))
        self.pending.update(zip(names, ended))
        return main

    def advance(self, name, values):
        try:
            self.pending[name] = self.chains[name].send(values)
        except StopIteration as end:
            self.results[name] = end.value
            del self.pending[name]

    def finish(self):
        while self.pending:
            self.point((), *self.pending)


def ungroup(parts, which):
    return jnp.concatenate(
        [
            part[..., which * heads * HD : (which + 1) * heads * HD]
            for part, (_, heads) in zip(parts, HEAD_GROUPS)
        ],
        -1,
    )


def norm_parts(values):
    center = values - jnp.mean(values, -1, keepdims=True)
    spread = jnp.mean(center * center, -1, keepdims=True)
    scale = lax.rsqrt(spread + EPS)
    return center * scale, scale


def norm_grad(grad, hat, scale, gain):
    e = grad * gain
    return scale * (
        e - jnp.mean(e, -1, keepdims=True) - hat * jnp.mean(e * hat, -1, keepdims=True)
    )


def ein(spec, a, b):
    return jnp.einsum(spec, a, b, preferred_element_type=f32)


def token_sum(values):
    return jnp.sum(values.astype(f32), (0, 1))


def body(
    patches,
    key_mask,
    attn_norm_gain,
    attn_norm_bias,
    query_weight,
    query_bias,
    key_weight,
    value_weight,
    value_bias,
    out_weight,
    out_bias,
    mlp_norm_gain,
    mlp_norm_bias,
    up_weight,
    up_bias,
    down_weight,
    down_bias,
    cotangent,
):
    rows, local, width = patches.shape
    group = SEQ // local
    share = rows // group
    shard = lax.axis_index("fsdp")
    seq = lax.axis_index("seq")
    member = seq % group

    flow = Flow()
    inputs_low = tokens_to_images(patches, group)

    small = [
        attn_norm_gain,
        attn_norm_bias,
        query_bias,
        value_bias,
        out_bias,
        mlp_norm_gain,
        mlp_norm_bias,
        down_bias,
        up_bias,
    ]
    gathered = gather_small(jnp.concatenate(small)).astype(f32)
    starts = [0]
    for v in small:
        starts.append(starts[-1] + v.shape[0])
    (
        first_gain,
        first_shift,
        query_shift,
        value_shift,
        out_shift,
        second_gain,
        second_shift,
        down_shift,
        up_shift,
    ) = (gathered[:, a:b].reshape(-1) for a, b in zip(starts[:-1], starts[1:]))

    def whole(weight):
        return lax.all_gather(weight, "fsdp", axis=0, tiled=True)

    project_full = whole(jnp.concatenate([query_weight, key_weight, value_weight], 1))
    project_shift = jnp.concatenate([query_shift, jnp.zeros_like(query_shift), value_shift])
    inputs_low, out_local = lax.optimization_barrier((inputs_low, out_weight))
    flow.start("out_weight", gather_chain(out_local))
    up_full = whole(up_weight)
    down_full = whole(down_weight.T)

    image_mask = lax.dynamic_slice(
        key_mask, (member * share, (seq // group) * SEQ), (share, SEQ)
    )
    key_keep = image_mask[:, None, :]

    inputs = inputs_low.astype(f32)
    hat_one, _ = norm_parts(inputs)
    normed_one = (hat_one * first_gain + first_shift).astype(bf16)
    projected = (ein("itd,dm->imt", normed_one, project_full) + project_shift[:, None]).astype(
        bf16
    )
    projected, cotangent = flow.point((projected, cotangent), "out_weight")
    cotangent_low = tokens_to_images(cotangent, group)
    context, lse = attend_forward(projected, key_keep)
    if "out_weight" in flow.pending:
        context, lse = flow.point((context, lse), "out_weight")
    out_full = flow.results["out_weight"]
    hidden = inputs + ein("int,nd->itd", context, out_full) + out_shift
    hat_two, scale_two = norm_parts(hidden)
    normed_two = (hat_two * second_gain + second_shift).astype(bf16)
    pre = ein("itd,df->itf", normed_two, up_full) + up_shift
    square = pre * pre
    tanh = jnp.tanh(pre * (GELU_A + GELU_B * square))
    half_pre = 0.5 * pre
    active, slope = lax.optimization_barrier(
        (
            (half_pre + half_pre * tanh).astype(bf16),
            (
                0.5 + 0.5 * tanh + half_pre * (1.0 - tanh * tanh) * (GELU_A + 3 * GELU_B * square)
            ).astype(bf16),
        )
    )
    out_grad_low = jnp.where(image_mask[:, :, None] > 0, cotangent_low, 0).astype(bf16)
    down_grad = rows_first(ein("itd,itf->df", out_grad_low, active).astype(bf16))
    down_bias_grad = token_sum(out_grad_low)
    active, slope, out_grad_low, down_grad = flow.point((active, slope, out_grad_low, down_grad))
    flow.start("down", reduce_chain([down_grad], group, (1,)))
    output = (hidden + ein("itf,df->itd", active, down_full) + down_shift).astype(bf16)
    output, slope = flow.point((output, slope))
    output = images_to_tokens(output, group)
    pre_grad = (ein("itd,df->itf", out_grad_low, down_full) * slope.astype(f32)).astype(bf16)
    up_bias_grad = token_sum(pre_grad)
    up_grad = rows_first(ein("itd,itf->df", normed_two, pre_grad).astype(bf16))
    pre_grad, up_grad, output = flow.point((pre_grad, up_grad, output), "down")
    flow.start("up", reduce_chain([up_grad], group, (1, 2)))
    normed_two_grad = ein("itf,df->itd", pre_grad, up_full)
    scaled_grad = normed_two_grad * second_gain
    norm_sums = (
        jnp.mean(scaled_grad, -1, keepdims=True),
        jnp.mean(scaled_grad * hat_two, -1, keepdims=True),
        jnp.sum(normed_two_grad * hat_two, (0, 1)),
        jnp.sum(normed_two_grad, (0, 1)),
    )
    normed_two_grad, norm_sums, output = flow.point((normed_two_grad, norm_sums, output), "down")
    mean_grad, mean_hat_grad, second_gain_grad, second_shift_grad = norm_sums
    hidden_grad = out_grad_low.astype(f32) + scale_two * (
        normed_two_grad * second_gain - mean_grad - hat_two * mean_hat_grad
    )

    attn_grad_low = hidden_grad.astype(bf16)
    context_grad = with_layout_constraint(
        ein("nd,itd->int", out_full, attn_grad_low).astype(bf16), Layout((0, 1, 2))
    )
    out_grad = rows_first(ein("int,itd->nd", context, attn_grad_low).astype(bf16))
    context_grad, out_grad = flow.point((context_grad, out_grad), "down")
    grads, parts = None, []
    per_group = HEAD_GROUPS[0][1] // STEP_HEADS
    points = (("up",), (), ("down",), ("up",))
    for step in range(len(HEAD_GROUPS) * per_group):
        number, inside = divmod(step, per_group)
        grads, part = attend_backward(
            projected,
            context,
            context_grad,
            lse,
            key_keep,
            step,
            HEAD_GROUPS[number],
            grads,
            part if inside else None,
        )
        if step == 3:
            out_bias_grad = token_sum(attn_grad_low)
            bias_grads = [jnp.sum(parts[0].astype(f32), (0, 2))]
            part, out_bias_grad, bias_grads = lax.optimization_barrier(
                (part, out_bias_grad, bias_grads)
            )
        grads, part, context_grad, attn_grad_low, parts = flow.point(
            (grads, part, context_grad, attn_grad_low, parts), *points[step]
        )
        if inside == per_group - 1:
            part = part.reshape(part.shape[0], -1, SEQ)
            parts.append(part)
            weight_grad = rows_first(ein("itd,imt->dm", normed_one, part).astype(bf16))
            grads, weight_grad, context_grad = flow.point(
                (grads, weight_grad, context_grad), *(["out_a"] if number else ["up"])
            )
            if number:
                flow.start("b", reduce_chain([weight_grad], group))
            else:
                flow.start("out_a", reduce_chain([out_grad, weight_grad], group, (1,)))
    bias_grads.append(jnp.sum(parts[1].astype(f32), (0, 2)))
    normed_one_grad = ein("imt,dm->itd", grads.reshape(projected.shape), project_full)
    query_bias_grad, value_bias_grad = ungroup(bias_grads, 0), ungroup(bias_grads, 2)
    hat_one, scale_one = norm_parts(inputs_low.astype(f32))
    first_gain_grad = jnp.sum(normed_one_grad * hat_one, (0, 1))
    first_shift_grad = jnp.sum(normed_one_grad, (0, 1))
    input_grad = (
        hidden_grad + norm_grad(normed_one_grad, hat_one, scale_one, first_gain)
    ).astype(bf16)
    small_grads = [
        first_gain_grad,
        first_shift_grad,
        query_bias_grad,
        value_bias_grad,
        out_bias_grad,
        second_gain_grad,
        second_shift_grad,
        down_bias_grad,
        up_bias_grad,
    ]
    input_grad, small_grads = flow.point(
        (input_grad, small_grads), "down", "up", "out_a", "b"
    )
    input_grad = images_to_tokens(input_grad, group)
    count = lax.axis_size("fsdp")
    packed = jnp.concatenate([v.reshape(count, -1) for v in small_grads], 1)
    flow.start("small", sum_chain(packed, group))
    flow.point((), "out_a", "b", "small")
    input_grad = flow.point(input_grad, *flow.pending)
    flow.finish()
    sums = flow.results
    (up_owned,), (down_owned,), (out_owned, part_a), (part_b,) = (
        sums[name] for name in ("up", "down", "out_a", "b")
    )
    down_owned = down_owned.T
    query_owned, key_owned, value_owned = (
        ungroup([part_a, part_b], which) for which in range(3)
    )

    packed = take_block(sums["small"], shard, 1)[0]
    (
        first_gain_owned,
        first_shift_owned,
        query_bias_owned,
        value_bias_owned,
        out_bias_owned,
        second_gain_owned,
        second_shift_owned,
        down_bias_owned,
        up_bias_owned,
    ) = (packed[a:b] for a, b in zip(starts[:-1], starts[1:]))
    return (
        output,
        input_grad,
        first_gain_owned,
        first_shift_owned,
        query_owned,
        query_bias_owned,
        key_owned,
        value_owned,
        value_bias_owned,
        out_owned,
        out_bias_owned,
        second_gain_owned,
        second_shift_owned,
        up_owned,
        up_bias_owned,
        down_owned,
        down_bias_owned,
    )


def solution(mesh):
    tokens, vector, matrix = P("fsdp", "seq", None), P("fsdp"), P("fsdp", None)
    in_specs = (
        tokens,
        matrix,
        vector,
        vector,
        matrix,
        vector,
        matrix,
        matrix,
        vector,
        matrix,
        vector,
        vector,
        vector,
        matrix,
        vector,
        P(None, "fsdp"),
        vector,
        tokens,
    )
    out_specs = (
        tokens,
        tokens,
        vector,
        vector,
        matrix,
        vector,
        matrix,
        matrix,
        vector,
        matrix,
        vector,
        vector,
        vector,
        matrix,
        vector,
        P(None, "fsdp"),
        vector,
    )
    return jax.shard_map(body, mesh=mesh, in_specs=in_specs, out_specs=out_specs, check_vma=False)
```
